256 devices in a mesh: leaf: 16 (over x, y), blk: 16 (over z, core).
Axes of the slice: x: 4, y: 4, z: 8, core: 2. Of those that a mesh axis runs over, the one named last changes fastest.
Arguments:
- near_tiles: bfloat16 [128, 16, 512, 512], P('leaf', 'blk'), may hold values from -0.25 to 0.25
- near_cols: int32 [128, 16], P('leaf', 'blk'), may hold values from 0 to 127, as said below
- near_count: int32 [128], P('leaf'), may hold values from 1 to 16, as said below
- probes: bfloat16 [128, 512, 512], P('leaf'), may hold values from -6 to 6
- mixing: float32 [512, 64], replicated, may hold values from -0.25 to 0.25
- far_tiles: bfloat16 [128, 16, 512, 512], P('leaf', 'blk'), may hold values from -6 to 6
- far_cols: int32 [128, 16], P('leaf', 'blk'), may hold values from 0 to 127, as said below
Outputs:
- coupling: float32 [128, 16, 64, 64], P('leaf', 'blk')
- root_part: float32 [128, 64, 64], P('leaf')
The draws below stay inside these ranges and needn't reach their ends.
Inputs may be any that keep to these rules, and one draw needn't show every extreme that they name: near_cols[r, k] lies within 8 of r; the slots below near_count[r] name distinct clusters. Slots at or past near_count[r] hold arbitrary tiles that must be ignored. far_cols[r, j] differs from r by more than 8.
All inputs are finite; a program needn't handle non-finite values.
Results may differ from the reference program's by a relative error of at most 0.0041.
Values may be sent and summed in bfloat16 or wider, within the bound.
No kernel may reach another device: no remote copies, remote signals or barrier semaphores. Data moves between devices by JAX's collectives and lax.ppermute only.
A program may use at most 128 MiB of HBM per device.

```python
import math
import jax
import jax.numpy as jnp
from jax import lax

B = 512
RANK = 64
P_SIZE = 512
RC_DEV = 8
REACH = 8
CLUSTERS = 128
NEAR = 16
FAR = 16
N_LEAF = 16


def draw_near_cols(key, part):
    window_size = 2 * REACH + 1
    offsets = jnp.arange(window_size) - REACH
    row_ids = jnp.arange(CLUSTERS)[:, None]
    target = row_ids + offsets[None, :]
    inside = (target >= 0) & (target < CLUSTERS)
    scores = jax.random.randint(key, (CLUSTERS, window_size), 0, 1 << 20) * 64 + jnp.arange(window_size)[None, :]
    scores = jnp.where(inside, scores, scores + (1 << 27))
    ordering = jnp.argsort(scores, axis=1, stable=True)[:, :NEAR]
    picked = jnp.take_along_axis(target, ordering, axis=1)
    return jnp.clip(picked, 0, CLUSTERS - 1).astype(jnp.int32)


def draw_near_count(key, part):
    first_key, second_key, third_key = jax.random.split(key, 3)
    row_ids = jnp.arange(CLUSTERS)
    base_count = jax.random.randint(first_key, (CLUSTERS,), 1, NEAR // 2 + 1)
    dense_count = jax.random.randint(second_key, (CLUSTERS,), 3 * NEAR // 4, NEAR + 1)
    dense_start = jax.random.randint(third_key, (), REACH, CLUSTERS - REACH - CLUSTERS // 4 + 1)
    inside = (row_ids >= dense_start) & (row_ids < dense_start + CLUSTERS // 4)
    counts = jnp.where(inside, dense_count, base_count)
    counts = jnp.where(row_ids == dense_start, NEAR, counts)
    valid_count = jnp.minimum(row_ids, REACH) + jnp.minimum(CLUSTERS - 1 - row_ids, REACH) + 1
    return jnp.minimum(counts, valid_count).astype(jnp.int32)


def draw_far_cols(key, part):
    row_ids = jnp.arange(CLUSTERS)[:, None]
    distance = jax.random.randint(key, (CLUSTERS, FAR), REACH + 1, CLUSTERS - REACH)
    return ((row_ids + distance) % CLUSTERS).astype(jnp.int32)


def block_scale(own_key, extent, cuts, smallest, largest):
    def one(position, blocks):
        draws = jax.random.uniform(jax.random.fold_in(jax.random.fold_in(own_key, 6), position), (blocks,), jnp.float32, smallest / len(cuts), largest / len(cuts))
        return jnp.repeat(jnp.exp(draws), extent[position] // blocks).reshape((-1,) + (1,) * (len(extent) - position - 1))

    level = one(*cuts[0])
    for cut in cuts[1:]:
        level = level * one(*cut)
    return level


def gaussian(rng, extent, spread, bound, pieces=(), kind=jnp.bfloat16):
    array = spread * jax.random.normal(rng, extent, jnp.float32)
    if pieces:
        array = array * block_scale(rng, extent, pieces, -0.22, 0.18)
    return jnp.clip(array, -bound, bound).astype(kind)


def setup_inputs(seed: int = 0) -> dict:
    key_list = jax.random.split(jax.random.key(seed), 8)
    near_tiles = gaussian(key_list[0], (CLUSTERS, NEAR, B, B), B ** -0.5, 0.25, ((0, 16), (1, 16)))
    near_cols = draw_near_cols(jax.random.fold_in(key_list[7], 71), 0)
    near_count = draw_near_count(jax.random.fold_in(key_list[7], 71), 0)
    probes = gaussian(key_list[3], (CLUSTERS, B, P_SIZE), 1.0, 6.0, ((0, 16),))
    mixing = gaussian(key_list[4], (P_SIZE, RANK), P_SIZE ** -0.5, 0.25, (), jnp.float32)
    far_tiles = gaussian(key_list[5], (CLUSTERS, FAR, B, B), 1.0, 6.0, ((0, 16), (1, 16)))
    far_cols = draw_far_cols(jax.random.fold_in(key_list[7], 71), 0)
    return dict(near_tiles=near_tiles, near_cols=near_cols, near_count=near_count, probes=probes, mixing=mixing, far_tiles=far_tiles, far_cols=far_cols)


highest = lax.Precision.HIGHEST

def basis_from(gram_matrix, mixed_rows):
    lower_factor = jnp.linalg.cholesky(gram_matrix)
    solved = jax.scipy.linalg.solve_triangular(lower_factor, jnp.swapaxes(mixed_rows, -1, -2), lower=True)
    return jnp.swapaxes(solved, -1, -2)

def merge(stacked, mixing):
    mixed_rows = jnp.einsum('...mp,pk->...mk', stacked, mixing, precision=highest)
    gram_matrix = jnp.einsum('...mk,...ml->...kl', mixed_rows, mixed_rows, precision=highest)
    transfer = basis_from(gram_matrix, mixed_rows)
    merged = jnp.einsum('...mk,...mp->...kp', transfer, stacked, precision=highest)
    return (transfer, merged)

def reference(near_tiles, near_cols, near_count, probes, mixing, far_tiles, far_cols):
    slot_ids = jnp.arange(near_cols.shape[1])

    def leaf_sketch(operands):
        row_tiles, row_cols, row_count = operands
        gathered = probes[row_cols].astype(jnp.float32)
        products = jnp.einsum('kab,kbp->kap', row_tiles.astype(jnp.float32), gathered)
        keep_mask = (slot_ids < row_count).astype(products.dtype)
        return jnp.einsum('k,kap->ap', keep_mask, products)
    sketch = lax.map(leaf_sketch, (near_tiles, near_cols, near_count))
    compressed = jnp.einsum('rbp,pk->rbk', sketch, mixing, precision=highest)
    gram_matrix = jnp.einsum('rbk,rbl->rkl', compressed, compressed, precision=highest)
    leaf_basis = basis_from(gram_matrix, compressed)
    leaf_proj = jnp.einsum('rbk,rbp->rkp', leaf_basis, sketch, precision=highest)
    basis_low = leaf_basis.astype(jnp.bfloat16)

    def couple(operands):
        row_tiles, row_cols, own_basis = operands
        far_image = jnp.einsum('jab,jbk->jak', row_tiles.astype(jnp.float32), basis_low[row_cols].astype(jnp.float32))
        return jnp.einsum('ak,jal->jkl', own_basis.astype(jnp.float32), far_image, precision=highest)
    coupling = lax.map(couple, (far_tiles, far_cols, basis_low))
    sub_stack = leaf_proj.reshape(N_LEAF, RC_DEV * RANK, leaf_proj.shape[2])
    sub_transfer, node_sketches = merge(sub_stack, mixing)
    levels = N_LEAF.bit_length() - 1
    path_factor = jnp.broadcast_to(jnp.eye(RANK, dtype=jnp.float32), (N_LEAF, RANK, RANK))
    subtree_ids = jnp.arange(N_LEAF)
    for depth_index in range(levels):
        paired = node_sketches.reshape(node_sketches.shape[0] // 2, 2 * RANK, node_sketches.shape[2])
        transfer, node_sketches = merge(paired, mixing)
        halves = transfer.reshape(transfer.shape[0], 2, RANK, RANK)
        picked = halves[subtree_ids >> depth_index + 1, subtree_ids >> depth_index & 1]
        path_factor = jnp.einsum('gab,gbc->gac', path_factor, picked, precision=highest)
    sub_blocks = sub_transfer.reshape(N_LEAF, RC_DEV, RANK, RANK)
    root_part = jnp.einsum('gcab,gbd->gcad', sub_blocks, path_factor, precision=highest)
    root_part = root_part.reshape(N_LEAF * RC_DEV, RANK, RANK) * math.sqrt(N_LEAF * RC_DEV * RANK)
    return (coupling, root_part)
```

```python
import functools
import math

import jax
import jax.numpy as jnp
from jax import lax
from jax.experimental import pallas as pl
from jax.experimental.pallas import tpu as pltpu
from jax.sharding import PartitionSpec as P

RANK = 64
REACH = 8
LANES = 128

f32 = jnp.float32
bf16 = jnp.bfloat16
highest = lax.Precision.HIGHEST

NN = (((1,), (0,)), ((), ()))
NT = (((1,), (1,)), ((), ()))
TN = (((0,), (0,)), ((), ()))


def dot(a, b, dims, precision=None):
    return lax.dot_general(a, b, dims, precision=precision, preferred_element_type=f32)


def pieces(x):
    high = x.astype(bf16)
    rest = x - high.astype(f32)
    middle = rest.astype(bf16)
    low = (rest - middle.astype(f32)).astype(bf16)
    return high, middle, low


def stacked_dot(stack, other, dims):
    full = dot(stack, other, dims)
    rows = full.shape[0] // 3
    return full[:rows] + full[rows : 2 * rows] + full[2 * rows :]


def factor(gram):
    n = gram.shape[0]
    row = lax.broadcasted_iota(jnp.int32, (n, n), 0)
    col = lax.broadcasted_iota(jnp.int32, (n, n), 1)
    tall = lax.broadcasted_iota(jnp.int32, (n, 1), 0)
    work = jnp.concatenate([gram, (row == col).astype(f32)], axis=1)
    scales = jnp.zeros((n, 1), f32)
    for j in range(n):
        pivot = work[j : j + 1, j : j + 1]
        scales = jnp.where(tall == j, pivot, scales)
        if j < n - 1:
            multiplier = jnp.where(tall > j, work[:, j : j + 1] / pivot, 0.0)
            work = work - multiplier * work[j : j + 1, :]
    work = work * (1.0 / jnp.sqrt(scales))
    upper = jnp.where(col >= row, work[:, :n], 0.0)
    return upper, work[:, n:]


def mixed_probes_kernel(half_ref, mixing_ref, probes_ref, out_ref, stack_ref):
    del half_ref

    @pl.when(pl.program_id(0) == 0)
    def _():
        stack_ref[...] = jnp.concatenate(pieces(mixing_ref[...].T), axis=0)

    out_ref[0] = stacked_dot(stack_ref[...], probes_ref[0], NT)


def mixed_probes(half, mixing, probes):
    count, rows, width = probes.shape
    part = count // 2
    return pl.pallas_call(
        mixed_probes_kernel,
        out_shape=jax.ShapeDtypeStruct((part, RANK, rows), f32),
        grid_spec=pltpu.PrefetchScalarGridSpec(
            num_scalar_prefetch=1,
            grid=(part,),
            in_specs=[
                pl.BlockSpec((width, RANK), lambda i, half: (0, 0)),
                pl.BlockSpec((1, rows, width), lambda i, half: (half[0] * part + i, 0, 0)),
            ],
            out_specs=pl.BlockSpec((1, RANK, rows), lambda i, half: (i, 0, 0)),
            scratch_shapes=[pltpu.VMEM((3 * RANK, width), bf16)],
        ),
        cost_estimate=pl.CostEstimate(
            flops=2 * part * rows * width * 3 * RANK,
            bytes_accessed=part * rows * (2 * width + 4 * RANK),
            transcendentals=0,
        ),
        name="mixed_probes",
    )(half, mixing, probes)


def sketch_kernel(
    meta_ref, own_a, own_b, before_a, before_b, after_a, after_b, tile_ref, keep_ref, send_ref, pick_ref
):
    i = pl.program_id(0)
    count = pl.num_programs(0)
    part = own_a.shape[0]
    core = meta_ref[2 * count]
    column = jnp.clip(meta_ref[i], 0, 6 * part - 1)
    segment = column // (2 * part)
    inner = column % (2 * part)
    mine = inner // part == core
    place = inner % part
    sources = ((before_a, before_b), (own_a, own_b), (after_a, after_b))
    for s, (first, second) in enumerate(sources):

        @pl.when((segment == s) & mine)
        def _():
            pick_ref[...] = first[place]

        @pl.when((segment == s) & jnp.logical_not(mine))
        def _():
            pick_ref[...] = second[place]

    stack = jnp.concatenate(pieces(pick_ref[...]), axis=0)
    mixed = stacked_dot(stack, tile_ref[0, 0], NT)
    mixed = jnp.where(meta_ref[count + i] > 0, mixed, 0.0)
    width = mixed.shape[1] // 2

    @pl.when(core == 0)
    def _():
        keep_ref[0] = mixed[:, :width]
        send_ref[0] = mixed[:, width:]

    @pl.when(core != 0)
    def _():
        keep_ref[0] = mixed[:, width:]
        send_ref[0] = mixed[:, :width]


def compress(meta, parts, near_tiles):
    count, _, rows, width = near_tiles.shape
    whole = pl.BlockSpec((count // 2, RANK, width), lambda i, meta: (0, 0, 0), pipeline_mode=pl.Buffered(1))
    half = pl.BlockSpec((1, RANK, rows // 2), lambda i, meta: (i, 0, 0))
    shape = jax.ShapeDtypeStruct((count, RANK, rows // 2), f32)
    return pl.pallas_call(
        sketch_kernel,
        out_shape=(shape, shape),
        grid_spec=pltpu.PrefetchScalarGridSpec(
            num_scalar_prefetch=1,
            grid=(count,),
            in_specs=[whole] * 6 + [pl.BlockSpec((1, 1, rows, width), lambda i, meta: (i, 0, 0, 0))],
            out_specs=(half, half),
            scratch_shapes=[pltpu.VMEM((RANK, width), f32)],
        ),
        cost_estimate=pl.CostEstimate(
            flops=2 * count * rows * width * 3 * RANK,
            bytes_accessed=count * rows * (2 * width + 16 * RANK),
            transcendentals=0,
        ),
        name="compress",
    )(meta, *parts, near_tiles)


def gram_kernel(terms_ref, mixed_ref, gram_ref):
    total = terms_ref[0]
    for k in range(1, terms_ref.shape[0]):
        total = total + terms_ref[k]
    mixed_ref[...] = total
    gram_ref[...] = dot(total, total, NT, highest)


def gram_of(terms):
    return pl.pallas_call(
        gram_kernel,
        out_shape=(
            jax.ShapeDtypeStruct(terms.shape[1:], f32),
            jax.ShapeDtypeStruct((RANK, RANK), f32),
        ),
        name="gram",
    )(terms)


def basis_kernel(core_ref, mixed_ref, gram_ref, other_ref, out_ref):
    upper, inverse = factor(gram_ref[...] + other_ref[...])
    basis = dot(inverse, mixed_ref[...], NN, highest)
    half = RANK // 2
    rows = jnp.where(core_ref[0] == 0, upper[:half], upper[half:])
    high = rows.astype(bf16).astype(f32)
    middle = (rows - high).astype(bf16).astype(f32)
    low = rows - high - middle
    left = jnp.concatenate([high, middle], axis=0)
    right = jnp.concatenate([low, jnp.zeros_like(low)], axis=0)
    block = jnp.concatenate([basis, left, right], axis=1).astype(bf16)
    for k in range(out_ref.shape[0]):
        out_ref[k] = block


def basis_of(core, mixed, gram, other, copies):
    vmem = pl.BlockSpec(memory_space=pltpu.VMEM)
    return pl.pallas_call(
        basis_kernel,
        out_shape=jax.ShapeDtypeStruct((copies, RANK, mixed.shape[1] + LANES), bf16),
        in_specs=[pl.BlockSpec(memory_space=pltpu.SMEM), vmem, vmem, vmem],
        out_specs=vmem,
        name="basis",
    )(core, mixed, gram, other)


def spread_kernel(meta_ref, own_ref, other_ref, out_ref, basis_ref, upper_ref, work_ref):
    count = own_ref.shape[0]
    groups = out_ref.shape[0] // count
    blocks = RANK // groups
    width = own_ref.shape[2] - LANES
    half = RANK // 2
    tiles = work_ref.shape[0]
    first = meta_ref[count] == 0
    total = jnp.zeros((RANK, RANK), f32)
    for r in range(count):
        mine, others = own_ref[r].astype(f32), other_ref[r].astype(f32)
        sides = (jnp.where(first, mine, others), jnp.where(first, others, mine))
        uppers = []
        for h, side in enumerate(sides):
            basis_ref[r, :, h * width : (h + 1) * width] = side[:, :width].astype(bf16)
            for q in range(blocks):
                for t in range(width // LANES):
                    work_ref[(q * 2 + h) * width // LANES + t, pl.ds(r, groups, stride=count), :] = side[
                        q * groups : (q + 1) * groups, t * LANES : (t + 1) * LANES
                    ]
            uppers.append(
                side[:half, width : width + RANK]
                + side[half:, width : width + RANK]
                + side[:half, width + RANK :]
            )
        upper = jnp.concatenate(uppers, axis=0)
        upper_ref[r] = upper
        total = total + dot(upper, upper, TN, highest)
        work_ref[tiles - 2, pl.ds(r, groups, stride=count), :] = jnp.full(
            (groups, LANES), meta_ref[r].astype(f32), f32
        )
    work_ref[tiles - 1] = jnp.zeros((groups * count, LANES), f32)
    for p in range(2):
        low_row = 2 * p * groups
        packed = jnp.concatenate(
            [total[low_row : low_row + groups], total[low_row + groups : low_row + 2 * groups]], axis=1
        )
        for k, piece in enumerate(pieces(packed)):
            work_ref[tiles - 1, pl.ds(2 * k + p, groups, stride=count), :] = piece.astype(f32)
    for t in range(tiles):
        out_ref[:, t * LANES : (t + 1) * LANES] = work_ref[t].astype(bf16)


def spread(meta, own, other, groups):
    count, _, width = own.shape
    rows = 2 * (width - LANES)
    total = RANK // groups * rows + 2 * LANES
    vmem = pl.BlockSpec(memory_space=pltpu.VMEM)
    return pl.pallas_call(
        spread_kernel,
        out_shape=(
            jax.ShapeDtypeStruct((groups * count, total), bf16),
            jax.ShapeDtypeStruct((count, RANK, rows), bf16),
            jax.ShapeDtypeStruct((count, RANK, RANK), f32),
        ),
        in_specs=[pl.BlockSpec(memory_space=pltpu.SMEM), vmem, vmem],
        out_specs=(vmem, vmem, vmem),
        scratch_shapes=[pltpu.VMEM((total // LANES, groups * count, LANES), f32)],
        name="spread",
    )(meta, own, other)


def choose_kernel(count, in_ref, out_ref):
    clusters, total = in_ref.shape
    body = total - 2 * LANES
    wanted = in_ref[:, body : body + LANES].astype(f32)
    column = lax.broadcasted_iota(jnp.int32, (clusters, clusters), 1).astype(f32)
    select = (wanted == column).astype(bf16)
    out_ref[:, :body] = dot(select, in_ref[:, :body], NN).astype(bf16)
    row = lax.broadcasted_iota(jnp.int32, (count, clusters), 0)
    column = lax.broadcasted_iota(jnp.int32, (count, clusters), 1) % count
    gather = (((column == row) | (column == row + 2) | (column == row + 4)) & (row < 2)).astype(bf16)
    sums = dot(gather, in_ref[:, body + LANES :], NN)[:2]
    block = jnp.concatenate([piece.astype(f32) for piece in pieces(sums)] + [jnp.zeros((count - 6, LANES), f32)], axis=0)
    out_ref[:, body:] = jnp.concatenate([block] * (clusters // count), axis=0).astype(bf16)


def choose(received, count):
    rows, total = received.shape
    return pl.pallas_call(
        functools.partial(choose_kernel, count),
        out_shape=jax.ShapeDtypeStruct((rows, total - LANES), bf16),
        name="choose",
    )(received)


def couple_kernel(scale, basis_ref, upper_ref, received_ref, tile_ref, coupling_ref, root_ref, work_ref):
    i = pl.program_id(0)
    count = upper_ref.shape[0]
    rows, total = received_ref.shape
    body = total - LANES
    groups = rows // count
    blocks = RANK // groups
    width = body // blocks
    tiles = work_ref.shape[0]

    @pl.when(i == 0)
    def _():
        for t in range(tiles):
            work_ref[t] = received_ref[:, t * LANES : (t + 1) * LANES].astype(f32)
        parts = []
        for p in range(2):
            packed = sum(work_ref[tiles - 1, pl.ds(2 * k + p, groups, stride=count), :] for k in range(3))
            parts += [packed[:, :RANK], packed[:, RANK:]]
        _, inverse = factor(jnp.concatenate(parts, axis=0))
        for r in range(count):
            root_ref[r] = dot(upper_ref[r], inverse, NT, highest) * scale

    image = dot(basis_ref[0], tile_ref[0, 0], NN)
    wide = width // LANES
    far = jnp.concatenate(
        [
            jnp.concatenate(
                [work_ref[q * wide + t, pl.ds(i, groups, stride=count), :] for t in range(wide)], axis=1
            ).astype(bf16)
            for q in range(blocks)
        ],
        axis=0,
    )
    coupling_ref[0, 0] = stacked_dot(jnp.concatenate(pieces(image), axis=0), far, NT)


def couple(basis, upper, received, far_tiles, scale):
    count, _, rows, width = far_tiles.shape
    return pl.pallas_call(
        functools.partial(couple_kernel, scale),
        out_shape=(
            jax.ShapeDtypeStruct((count, 1, RANK, RANK), f32),
            jax.ShapeDtypeStruct((count, RANK, RANK), f32),
        ),
        grid=(count,),
        in_specs=[
            pl.BlockSpec((1, RANK, rows), lambda i: (i, 0, 0)),
            pl.BlockSpec((count, RANK, RANK), lambda i: (0, 0, 0)),
            pl.BlockSpec(received.shape, lambda i: (0, 0)),
            pl.BlockSpec((1, 1, rows, width), lambda i: (i, 0, 0, 0)),
        ],
        out_specs=(
            pl.BlockSpec((1, 1, RANK, RANK), lambda i: (i, 0, 0, 0)),
            pl.BlockSpec((count, RANK, RANK), lambda i: (0, 0, 0)),
        ),
        scratch_shapes=[pltpu.VMEM((received.shape[1] // LANES, received.shape[0], LANES), f32)],
        name="couple",
    )(basis, upper, received, far_tiles)


def shards(near_tiles, near_cols, near_count, probes, mixing, far_tiles, far_cols):
    count = probes.shape[0]
    subtrees = lax.axis_size("leaf")
    members = lax.axis_size("blk")
    leaf_pos = lax.axis_index("leaf")
    blk_pos = lax.axis_index("blk")
    core = blk_pos % 2
    up = [(i, i + 1) for i in range(subtrees - 1)]
    down = [(j, i) for i, j in up]
    pair = [(i, i ^ 1) for i in range(members)]
    lanes = [list(range(c, members, 2)) for c in range(2)]

    core_vec = core.reshape(1).astype(jnp.int32)
    live = (blk_pos < near_count).astype(jnp.int32)
    near_meta = jnp.concatenate([near_cols[:, 0] - (leaf_pos * count - REACH), live, core_vec])
    far_meta = jnp.concatenate([far_cols[:, 0], core_vec])

    own_a = mixed_probes(core_vec, mixing, probes)
    before_a = lax.ppermute(own_a, "leaf", up)
    after_a = lax.ppermute(own_a, "leaf", down)
    own_b = mixed_probes(1 - core_vec, mixing, probes)
    before_b = lax.ppermute(before_a, "blk", pair)
    after_b = lax.ppermute(after_a, "blk", pair)
    keep, send = compress(near_meta, (own_a, own_b, before_a, before_b, after_a, after_b), near_tiles)
    halves = keep + lax.ppermute(send, "blk", pair)
    terms = lax.all_to_all(halves, "blk", 0, 0, tiled=True, axis_index_groups=lanes)
    mixed, gram = gram_of(terms)
    own = basis_of(core_vec, mixed, gram, lax.ppermute(gram, "blk", pair), count)
    own = lax.all_to_all(own, "blk", 0, 0, tiled=True, axis_index_groups=lanes)
    other = lax.ppermute(own, "blk", pair)
    payload, basis, upper = spread(far_meta, own, other, subtrees)
    slices = lax.all_to_all(payload.reshape(subtrees, count, -1), "leaf", 0, 0, tiled=True)
    chosen = choose(slices.reshape(payload.shape), count)
    received = lax.all_to_all(chosen.reshape(subtrees, count, -1), "leaf", 0, 0, tiled=True)
    scale = math.sqrt(subtrees * count * RANK)
    return couple(basis, upper, received.reshape(chosen.shape), far_tiles, scale)


def solution(mesh):
    in_specs = (
        P("leaf", "blk", None, None),
        P("leaf", "blk"),
        P("leaf"),
        P("leaf", None, None),
        P(),
        P("leaf", "blk", None, None),
        P("leaf", "blk"),
    )
    out_specs = (P("leaf", "blk", None, None), P("leaf", None, None))
    return jax.shard_map(shards, mesh=mesh, in_specs=in_specs, out_specs=out_specs, check_vma=False)
```

```python
import functools
import math

import jax
import jax.numpy as jnp
from jax import lax
from jax.experimental import pallas as pl
from jax.experimental.pallas import tpu as pltpu
from jax.sharding import PartitionSpec as P

RANK = 64
REACH = 8
LANES = 128
PANEL = 8

f32 = jnp.float32
bf16 = jnp.bfloat16
highest = lax.Precision.HIGHEST

HBM = pl.BlockSpec(memory_space=pltpu.HBM)
SMEM = pl.BlockSpec(memory_space=pltpu.SMEM)
VMEM = pl.BlockSpec(memory_space=pltpu.VMEM)

LIMIT = pltpu.CompilerParams(vmem_limit_bytes=24 << 20)

NN = (((1,), (0,)), ((), ()))
NT = (((1,), (1,)), ((), ()))
TN = (((0,), (0,)), ((), ()))


def dot(a, b, dims, precision=None):
    return lax.dot_general(a, b, dims, precision=precision, preferred_element_type=f32)


def pieces(x):
    high = x.astype(bf16)
    rest = x - high.astype(f32)
    middle = rest.astype(bf16)
    low = (rest - middle.astype(f32)).astype(bf16)
    return high, middle, low


def in_vmem(x):
    return pltpu.with_memory_space_constraint(x, pltpu.VMEM)


def factor(gram):
    n = gram.shape[0]
    row = lax.broadcasted_iota(jnp.int32, (n, n), 0)
    col = lax.broadcasted_iota(jnp.int32, (n, n), 1)
    tall = lax.broadcasted_iota(jnp.int32, (PANEL, 2 * n), 0)
    work = jnp.concatenate([gram, (row == col).astype(f32)], axis=1)
    panels = [work[k : k + PANEL] for k in range(0, n, PANEL)]
    for k in range(len(panels)):
        columns = [
            [
                jnp.broadcast_to(panels[t][:, k * PANEL + j : k * PANEL + j + 1], (PANEL, 2 * n))
                for j in range(PANEL)
            ]
            for t in range(k, len(panels))
        ]
        scales = jnp.zeros((PANEL, 2 * n), f32)
        for j in range(PANEL):
            inverse = 1.0 / columns[0][j][j : j + 1]
            scales = jnp.where(tall == j, inverse, scales)
            entries = [columns[0][i][j : j + 1] for i in range(PANEL)]
            pivot_row = panels[k][j : j + 1]
            for t in range(k, len(panels)):
                multiplier = columns[t - k][j] * inverse
                if t == k:
                    if j == PANEL - 1:
                        continue
                    multiplier = jnp.where(tall > j, multiplier, 0.0)
                for i in range(j + 1, PANEL):
                    columns[t - k][i] = columns[t - k][i] - multiplier * entries[i]
                panels[t] = panels[t] - multiplier * pivot_row
        panels[k] = panels[k] * jnp.sqrt(scales)
    work = jnp.concatenate(panels, axis=0)
    upper = jnp.where(col >= row, work[:, :n], 0.0)
    return upper, work[:, n:]


def weights_of(x):
    high, middle, low = (piece.astype(f32) for piece in pieces(x))
    lane = lax.broadcasted_iota(jnp.int32, x.shape, 1)
    return jnp.concatenate([jnp.where(lane < RANK, high, middle), low], axis=1).astype(bf16)


def weighted(x, weights):
    terms = dot(x, weights, NN)
    first, last = terms[:, :LANES], terms[:, LANES:]
    return first + pltpu.roll(first, RANK, 1) + last


def folded(x):
    rows = x.shape[0] // 2
    lane = lax.broadcasted_iota(jnp.int32, (rows, LANES), 1)
    return jnp.where(lane < RANK, x[:rows], x[rows:])


def unfolded(x):
    lane = lax.broadcasted_iota(jnp.int32, x.shape, 1)
    turned = pltpu.roll(x, RANK, 1)
    return jnp.concatenate([jnp.where(lane < RANK, x, turned), jnp.where(lane < RANK, turned, x)], axis=0)


def mixed_probes_kernel(half_ref, mixing_hbm, probes_ref, out_ref, mixing_ref, tiles_ref, sems):
    part = out_ref.shape[0]
    start = half_ref[0] * part
    first = pltpu.make_async_copy(mixing_hbm, mixing_ref, sems.at[part])
    copies = [pltpu.make_async_copy(probes_ref.at[start + i], tiles_ref.at[i], sems.at[i]) for i in range(part)]
    for copy in [first] + copies:
        copy.start()
    first.wait()
    mixing = mixing_ref[...]
    weights = weights_of(jnp.concatenate([mixing, mixing], axis=0).T)
    for i, copy in enumerate(copies):
        copy.wait()
        out_ref[i] = folded(weighted(tiles_ref[i], weights))


def mixed_probes(half, mixing, probes):
    count, rows, width = probes.shape
    part = count // 2
    return pl.pallas_call(
        mixed_probes_kernel,
        out_shape=pltpu.VMEM((part, rows // 2, LANES), f32),
        in_specs=[SMEM, HBM, HBM],
        out_specs=VMEM,
        scratch_shapes=[
            pltpu.VMEM(mixing.shape, f32),
            pltpu.VMEM((part, rows, width), bf16),
            pltpu.SemaphoreType.DMA((part + 1,)),
        ],
        cost_estimate=pl.CostEstimate(
            flops=2 * part * rows * width * 3 * RANK,
            bytes_accessed=part * rows * (2 * width + 4 * RANK),
            transcendentals=0,
        ),
        compiler_params=LIMIT,
        name="mixed_probes",
    )(half, mixing, probes)


def sketch_kernel(
    meta_ref, own_a, own_b, before_a, before_b, after_a, after_b, near_ref, keep_ref, send_ref, pick_ref
):
    count = near_ref.shape[0]
    part = own_a.shape[0]
    core = meta_ref[2 * count]

    def pick(i):
        column = jnp.clip(meta_ref[i], 0, 6 * part - 1)
        group = column // part
        place = column % part
        for s, sides in enumerate(((before_a, before_b), (own_a, own_b), (after_a, after_b))):
            for h, side in enumerate(sides):

                @pl.when(group == 2 * s + (core if h == 0 else 1 - core))
                def _():
                    pick_ref[i] = side[place]

    for i in range(count):
        pick(i)
    for i in range(count):
        mixed = folded(weighted(near_ref[i, 0], weights_of(unfolded(pick_ref[i]))))
        mixed = jnp.where(meta_ref[count + i] > 0, mixed, 0.0)
        rows = mixed.shape[0] // 2
        keep_ref[i] = jnp.where(core == 0, mixed[:rows], mixed[rows:])
        send_ref[i] = jnp.where(core == 0, mixed[rows:], mixed[:rows])


def compress(meta, parts, near_tiles):
    count, _, rows, width = near_tiles.shape
    shape = pltpu.VMEM((count, rows // 4, LANES), f32)
    return pl.pallas_call(
        sketch_kernel,
        out_shape=(shape, shape),
        in_specs=[SMEM] + [VMEM] * 7,
        out_specs=(VMEM, VMEM),
        scratch_shapes=[pltpu.VMEM((count, rows // 2, LANES), f32)],
        cost_estimate=pl.CostEstimate(
            flops=2 * count * rows * width * 3 * RANK,
            bytes_accessed=count * rows * (2 * width + 16 * RANK),
            transcendentals=0,
        ),
        compiler_params=LIMIT,
        name="compress",
    )(meta, *[in_vmem(part) for part in parts], in_vmem(near_tiles))


def gram_kernel(terms_ref, mixed_ref, gram_ref):
    total = terms_ref[0]
    for k in range(1, terms_ref.shape[0]):
        total = total + terms_ref[k]
    mixed = total.T
    mixed_ref[...] = mixed
    first, second = mixed[:RANK], mixed[RANK:]
    gram_ref[...] = dot(first, first, NT, highest) + dot(second, second, NT, highest)


def gram_of(terms):
    return pl.pallas_call(
        gram_kernel,
        out_shape=(
            pltpu.VMEM((terms.shape[2], terms.shape[1]), f32),
            pltpu.VMEM((RANK, RANK), f32),
        ),
        in_specs=[VMEM],
        out_specs=(VMEM, VMEM),
        compiler_params=LIMIT,
        name="gram",
    )(in_vmem(terms))


def basis_kernel(core_ref, mixed_ref, gram_ref, other_ref, out_ref):
    upper, inverse = factor(gram_ref[...] + other_ref[...])
    basis = [dot(inverse, mixed_ref[k : k + RANK], NN, highest) for k in (0, RANK)]
    half = RANK // 2
    rows = jnp.where(core_ref[0] == 0, upper[:half], upper[half:])
    high, middle, low = (piece.astype(f32) for piece in pieces(rows))
    left = jnp.concatenate([high, middle], axis=0)
    right = jnp.concatenate([low, jnp.zeros_like(low)], axis=0)
    block = jnp.concatenate(basis + [left, right], axis=1).astype(bf16)
    for k in range(out_ref.shape[0]):
        out_ref[k] = block


def basis_of(core, mixed, gram, other, copies):
    return pl.pallas_call(
        basis_kernel,
        out_shape=pltpu.VMEM((copies, RANK, 2 * mixed.shape[1] + LANES), bf16),
        in_specs=[SMEM, VMEM, VMEM, VMEM],
        out_specs=VMEM,
        compiler_params=LIMIT,
        name="basis",
    )(core, in_vmem(mixed), in_vmem(gram), in_vmem(other))


def spread_kernel(meta_ref, own_ref, other_ref, out_ref, basis_ref, upper_ref, work_ref):
    count = own_ref.shape[0]
    groups = out_ref.shape[0] // count
    blocks = RANK // groups
    width = own_ref.shape[2] - LANES
    half = RANK // 2
    tiles = work_ref.shape[0]
    first = meta_ref[count] == 0
    total = jnp.zeros((RANK, RANK), f32)
    for r in range(count):
        mine, others = own_ref[r].astype(f32), other_ref[r].astype(f32)
        sides = (jnp.where(first, mine, others), jnp.where(first, others, mine))
        uppers = []
        for h, side in enumerate(sides):
            for t in range(width // LANES):
                strip = side[:, t * LANES : (t + 1) * LANES]
                place = 2 * t + h
                basis_ref[r, :, place * LANES : (place + 1) * LANES] = strip.astype(bf16)
                for q in range(blocks):
                    work_ref[2 * q * width // LANES + place, pl.ds(r, groups, stride=count), :] = strip[
                        q * groups : (q + 1) * groups
                    ]
            uppers.append(
                side[:half, width : width + RANK]
                + side[half:, width : width + RANK]
                + side[:half, width + RANK :]
            )
        upper = jnp.concatenate(uppers, axis=0)
        upper_ref[r] = upper
        total = total + dot(upper, upper, TN, highest)
        work_ref[tiles - 2, pl.ds(r, groups, stride=count), :] = jnp.full(
            (groups, LANES), meta_ref[r].astype(f32), f32
        )
    work_ref[tiles - 1] = jnp.zeros((groups * count, LANES), f32)
    for p in range(2):
        low_row = 2 * p * groups
        packed = jnp.concatenate(
            [total[low_row : low_row + groups], total[low_row + groups : low_row + 2 * groups]], axis=1
        )
        for k, piece in enumerate(pieces(packed)):
            work_ref[tiles - 1, pl.ds(2 * k + p, groups, stride=count), :] = piece.astype(f32)
    for t in range(tiles):
        out_ref[:, t * LANES : (t + 1) * LANES] = work_ref[t].astype(bf16)


def spread(meta, own, other, groups):
    count, _, width = own.shape
    rows = 2 * (width - LANES)
    total = RANK // groups * rows + 2 * LANES
    return pl.pallas_call(
        spread_kernel,
        out_shape=(
            pltpu.VMEM((groups * count, total), bf16),
            pltpu.VMEM((count, RANK, rows), bf16),
            pltpu.VMEM((count, RANK, RANK), f32),
        ),
        in_specs=[SMEM, VMEM, VMEM],
        out_specs=(VMEM, VMEM, VMEM),
        scratch_shapes=[pltpu.VMEM((total // LANES, groups * count, LANES), f32)],
        compiler_params=LIMIT,
        name="spread",
    )(meta, in_vmem(own), in_vmem(other))


def choose_kernel(count, in_ref, out_ref):
    clusters, total = in_ref.shape
    body = total - 2 * LANES
    wanted = in_ref[:, body : body + LANES].astype(f32)
    column = lax.broadcasted_iota(jnp.int32, (clusters, clusters), 1).astype(f32)
    select = (wanted == column).astype(bf16)
    out_ref[:, :body] = dot(select, in_ref[:, :body], NN).astype(bf16)
    row = lax.broadcasted_iota(jnp.int32, (count, clusters), 0)
    column = lax.broadcasted_iota(jnp.int32, (count, clusters), 1) % count
    gather = (((column == row) | (column == row + 2) | (column == row + 4)) & (row < 2)).astype(bf16)
    sums = dot(gather, in_ref[:, body + LANES :], NN)[:2]
    block = jnp.concatenate([piece.astype(f32) for piece in pieces(sums)] + [jnp.zeros((count - 6, LANES), f32)], axis=0)
    out_ref[:, body:] = jnp.concatenate([block] * (clusters // count), axis=0).astype(bf16)


def choose(received, count):
    rows, total = received.shape
    return pl.pallas_call(
        functools.partial(choose_kernel, count),
        out_shape=pltpu.VMEM((rows, total - LANES), bf16),
        in_specs=[VMEM],
        out_specs=VMEM,
        compiler_params=LIMIT,
        name="choose",
    )(in_vmem(received))


def couple_kernel(
    scale, basis_ref, upper_ref, received_ref, far_ref, coupling_ref, root_ref, work_ref
):
    count = upper_ref.shape[0]
    rows, total = received_ref.shape
    groups = rows // count
    blocks = RANK // groups
    wide = (total - LANES) // blocks // LANES
    tiles = work_ref.shape[0]
    for t in range(tiles):
        work_ref[t] = received_ref[:, t * LANES : (t + 1) * LANES].astype(f32)
    parts = []
    for p in range(2):
        packed = sum(work_ref[tiles - 1, pl.ds(2 * k + p, groups, stride=count), :] for k in range(3))
        parts += [packed[:, :RANK], packed[:, RANK:]]
    _, inverse = factor(jnp.concatenate(parts, axis=0))
    for i in range(count):
        far = [
            jnp.concatenate(
                [work_ref[q * wide + t, pl.ds(i, groups, stride=count), :] for t in range(wide)], axis=1
            )
            for q in range(blocks)
        ]
        far = jnp.concatenate(far, axis=0).astype(bf16)
        image = dot(far_ref[i, 0], far, NT)
        terms = dot(basis_ref[i], jnp.concatenate(pieces(image), axis=1), NN)
        coupling_ref[i, 0] = terms[:, :RANK] + terms[:, RANK : 2 * RANK] + terms[:, 2 * RANK :]
    for r in range(count):
        root_ref[r] = dot(upper_ref[r], inverse, NT, highest) * scale


def couple(basis, upper, received, far_tiles, scale):
    count = far_tiles.shape[0]
    return pl.pallas_call(
        functools.partial(couple_kernel, scale),
        out_shape=(
            jax.ShapeDtypeStruct((count, 1, RANK, RANK), f32),
            jax.ShapeDtypeStruct((count, RANK, RANK), f32),
        ),
        in_specs=[VMEM] * 4,
        out_specs=(VMEM, VMEM),
        scratch_shapes=[pltpu.VMEM((received.shape[1] // LANES, received.shape[0], LANES), f32)],
        compiler_params=LIMIT,
        name="couple",
    )(in_vmem(basis), in_vmem(upper), in_vmem(received), in_vmem(far_tiles))


def shards(near_tiles, near_cols, near_count, probes, mixing, far_tiles, far_cols):
    count = probes.shape[0]
    subtrees = lax.axis_size("leaf")
    members = lax.axis_size("blk")
    leaf_pos = lax.axis_index("leaf")
    blk_pos = lax.axis_index("blk")
    core = blk_pos % 2
    up = [(i, i + 1) for i in range(subtrees - 1)]
    down = [(j, i) for i, j in up]
    pair = [(i, i ^ 1) for i in range(members)]
    lanes = [list(range(c, members, 2)) for c in range(2)]

    core_vec = core.reshape(1).astype(jnp.int32)
    live = (blk_pos < near_count).astype(jnp.int32)
    near_meta = jnp.concatenate([near_cols[:, 0] - (leaf_pos * count - REACH), live, core_vec])
    far_meta = jnp.concatenate([far_cols[:, 0], core_vec])

    mixing, probes = (pltpu.with_memory_space_constraint(x, pltpu.HBM) for x in (mixing.T, probes))
    own_a = mixed_probes(core_vec, mixing, probes)
    before_a = lax.ppermute(own_a, "leaf", up)
    after_a = lax.ppermute(own_a, "leaf", down)
    own_b = mixed_probes(1 - core_vec, mixing, probes)
    before_b = lax.ppermute(before_a, "blk", pair)
    after_b = lax.ppermute(after_a, "blk", pair)
    keep, send = compress(near_meta, (own_a, own_b, before_a, before_b, after_a, after_b), near_tiles)
    halves = keep + lax.ppermute(send, "blk", pair)
    terms = lax.all_to_all(halves, "blk", 0, 0, tiled=True, axis_index_groups=lanes)
    mixed, gram = gram_of(terms)
    own = basis_of(core_vec, mixed, gram, lax.ppermute(gram, "blk", pair), count)
    own = lax.all_to_all(own, "blk", 0, 0, tiled=True, axis_index_groups=lanes)
    other = lax.ppermute(own, "blk", pair)
    payload, basis, upper = spread(far_meta, own, other, subtrees)
    slices = lax.all_to_all(payload.reshape(subtrees, count, -1), "leaf", 0, 0, tiled=True)
    chosen = choose(slices.reshape(payload.shape), count)
    received = lax.all_to_all(chosen.reshape(subtrees, count, -1), "leaf", 0, 0, tiled=True)
    scale = math.sqrt(subtrees * count * RANK)
    return couple(basis, upper, received.reshape(chosen.shape), far_tiles, scale)


def solution(mesh):
    in_specs = (
        P("leaf", "blk", None, None),
        P("leaf", "blk"),
        P("leaf"),
        P("leaf", None, None),
        P(),
        P("leaf", "blk", None, None),
        P("leaf", "blk"),
    )
    out_specs = (P("leaf", "blk", None, None), P("leaf", None, None))
    return jax.shard_map(shards, mesh=mesh, in_specs=in_specs, out_specs=out_specs, check_vma=False)
```

```python
import functools
import math

import jax
import jax.numpy as jnp
from jax import lax
from jax.experimental import pallas as pl
from jax.experimental.pallas import tpu as pltpu
from jax.sharding import PartitionSpec as P

RANK = 64
REACH = 8
LANES = 128
PANEL = 8

f32 = jnp.float32
bf16 = jnp.bfloat16
highest = lax.Precision.HIGHEST

HBM = pl.BlockSpec(memory_space=pltpu.HBM)
SMEM = pl.BlockSpec(memory_space=pltpu.SMEM)
VMEM = pl.BlockSpec(memory_space=pltpu.VMEM)

LIMIT = pltpu.CompilerParams(vmem_limit_bytes=24 << 20)

NN = (((1,), (0,)), ((), ()))
NT = (((1,), (1,)), ((), ()))
TN = (((0,), (0,)), ((), ()))


def dot(a, b, dims, precision=None):
    return lax.dot_general(a, b, dims, precision=precision, preferred_element_type=f32)


def pieces(x):
    high = x.astype(bf16)
    rest = x - high.astype(f32)
    middle = rest.astype(bf16)
    low = (rest - middle.astype(f32)).astype(bf16)
    return high, middle, low


def in_vmem(x):
    return pltpu.with_memory_space_constraint(x, pltpu.VMEM)


def factor(gram):
    n = gram.shape[0]
    row = lax.broadcasted_iota(jnp.int32, (n, n), 0)
    col = lax.broadcasted_iota(jnp.int32, (n, n), 1)
    tall = lax.broadcasted_iota(jnp.int32, (PANEL, 2 * n), 0)
    work = jnp.concatenate([gram, (row == col).astype(f32)], axis=1)
    panels = [work[k : k + PANEL] for k in range(0, n, PANEL)]
    for k in range(len(panels)):
        columns = [
            [
                jnp.broadcast_to(panels[t][:, k * PANEL + j : k * PANEL + j + 1], (PANEL, 2 * n))
                for j in range(PANEL)
            ]
            for t in range(k, len(panels))
        ]
        scales = jnp.zeros((PANEL, 2 * n), f32)
        for j in range(PANEL):
            inverse = 1.0 / columns[0][j][j : j + 1]
            scales = jnp.where(tall == j, inverse, scales)
            entries = [columns[0][i][j : j + 1] for i in range(PANEL)]
            pivot_row = panels[k][j : j + 1]
            for t in range(k, len(panels)):
                multiplier = columns[t - k][j] * inverse
                if t == k:
                    if j == PANEL - 1:
                        continue
                    multiplier = jnp.where(tall > j, multiplier, 0.0)
                for i in range(j + 1, PANEL):
                    columns[t - k][i] = columns[t - k][i] - multiplier * entries[i]
                panels[t] = panels[t] - multiplier * pivot_row
        panels[k] = panels[k] * jnp.sqrt(scales)
    work = jnp.concatenate(panels, axis=0)
    upper = jnp.where(col >= row, work[:, :n], 0.0)
    return upper, work[:, n:]


def weights_of(x):
    high, middle, low = (piece.astype(f32) for piece in pieces(x))
    lane = lax.broadcasted_iota(jnp.int32, x.shape, 1)
    return jnp.concatenate([jnp.where(lane < RANK, high, middle), low], axis=1).astype(bf16)


def weighted(x, weights):
    terms = dot(x, weights, NN)
    first, last = terms[:, :LANES], terms[:, LANES:]
    return first + pltpu.roll(first, RANK, 1) + last


def folded(x):
    rows = x.shape[0] // 2
    lane = lax.broadcasted_iota(jnp.int32, (rows, LANES), 1)
    return jnp.where(lane < RANK, x[:rows], x[rows:])


def unfolded(x):
    lane = lax.broadcasted_iota(jnp.int32, x.shape, 1)
    turned = pltpu.roll(x, RANK, 1)
    return jnp.concatenate([jnp.where(lane < RANK, x, turned), jnp.where(lane < RANK, turned, x)], axis=0)


def mixed_probes_kernel(start, mixing_hbm, probes_ref, out_ref, mixing_ref, tiles_ref, sems):
    part = out_ref.shape[0]
    first = pltpu.make_async_copy(mixing_hbm, mixing_ref, sems.at[part])
    copies = [pltpu.make_async_copy(probes_ref.at[start + i], tiles_ref.at[i], sems.at[i]) for i in range(part)]
    for copy in [first] + copies:
        copy.start()
    first.wait()
    mixing = mixing_ref[...]
    weights = weights_of(jnp.concatenate([mixing, mixing], axis=0).T)
    for i, copy in enumerate(copies):
        copy.wait()
        out_ref[i] = folded(weighted(tiles_ref[i], weights))


def mixed_probes(start, part, mixing, probes):
    _, rows, width = probes.shape
    return pl.pallas_call(
        functools.partial(mixed_probes_kernel, start),
        out_shape=pltpu.VMEM((part, rows // 2, LANES), f32),
        in_specs=[HBM, HBM],
        out_specs=VMEM,
        scratch_shapes=[
            pltpu.VMEM(mixing.shape, f32),
            pltpu.VMEM((part, rows, width), bf16),
            pltpu.SemaphoreType.DMA((part + 1,)),
        ],
        cost_estimate=pl.CostEstimate(
            flops=2 * part * rows * width * 3 * RANK,
            bytes_accessed=part * rows * (2 * width + 4 * RANK),
            transcendentals=0,
        ),
        compiler_params=LIMIT,
        name="mixed_probes",
    )(mixing, probes)


def load_kernel(*refs):
    count = len(refs) // 2
    sems = refs[-1]
    copies = [
        pltpu.make_async_copy(refs[k], refs[count + k], sems.at[k]) for k in range(count)
    ]
    for copy in copies:
        copy.start()
    for copy in copies:
        copy.wait()


def load(after, *arrays):
    def kernel(after_ref, *refs):
        load_kernel(*refs)

    arrays = [pltpu.with_memory_space_constraint(x, pltpu.HBM) for x in arrays]
    return pl.pallas_call(
        kernel,
        out_shape=tuple(pltpu.VMEM(x.shape, x.dtype) for x in arrays),
        in_specs=[VMEM] + [HBM] * len(arrays),
        out_specs=(VMEM,) * len(arrays),
        scratch_shapes=[pltpu.SemaphoreType.DMA((len(arrays),))],
        cost_estimate=pl.CostEstimate(
            flops=0, bytes_accessed=2 * sum(x.size * x.dtype.itemsize for x in arrays), transcendentals=0
        ),
        compiler_params=LIMIT,
        name="load",
    )(in_vmem(after), *arrays)


def sketch_kernel(
    meta_ref, own_a, own_b, moved_a, moved_b, other_a, other_b, near_ref, keep_ref, send_ref, pick_ref
):
    count = near_ref.shape[0]
    part = own_a.shape[0]
    core = meta_ref[2 * count]
    sources = (
        (own_a, 2), (own_b, 3), (moved_a, 4 * core), (moved_b, 4 * core + 1),
        (other_a, 4 - 4 * core), (other_b, 5 - 4 * core),
    )

    def pick(i):
        column = jnp.clip(meta_ref[i], 0, 6 * part - 1)
        for source, group in sources:

            @pl.when(column // part == group)
            def _():
                pick_ref[i] = source[column % part]

    for i in range(count):
        pick(i)
    for i in range(count):
        mixed = folded(weighted(near_ref[i, 0], weights_of(unfolded(pick_ref[i]))))
        mixed = jnp.where(meta_ref[count + i] > 0, mixed, 0.0)
        rows = mixed.shape[0] // 2
        keep_ref[i] = jnp.where(core == 0, mixed[:rows], mixed[rows:])
        send_ref[i] = jnp.where(core == 0, mixed[rows:], mixed[:rows])


def compress(meta, parts, near_tiles):
    count, _, rows, width = near_tiles.shape
    shape = pltpu.VMEM((count, rows // 4, LANES), f32)
    return pl.pallas_call(
        sketch_kernel,
        out_shape=(shape, shape),
        in_specs=[SMEM] + [VMEM] * 7,
        out_specs=(VMEM, VMEM),
        scratch_shapes=[pltpu.VMEM((count, rows // 2, LANES), f32)],
        cost_estimate=pl.CostEstimate(
            flops=2 * count * rows * width * 3 * RANK,
            bytes_accessed=count * rows * (2 * width + 16 * RANK),
            transcendentals=0,
        ),
        compiler_params=LIMIT,
        name="compress",
    )(meta, *[in_vmem(part) for part in parts], in_vmem(near_tiles))


def gram_kernel(terms_ref, mixed_ref, gram_ref):
    total = terms_ref[0]
    for k in range(1, terms_ref.shape[0]):
        total = total + terms_ref[k]
    mixed = total.T
    mixed_ref[...] = mixed
    first, second = mixed[:RANK], mixed[RANK:]
    gram_ref[...] = dot(first, first, NT, highest) + dot(second, second, NT, highest)


def gram_of(terms):
    return pl.pallas_call(
        gram_kernel,
        out_shape=(
            pltpu.VMEM((terms.shape[2], terms.shape[1]), f32),
            pltpu.VMEM((RANK, RANK), f32),
        ),
        in_specs=[VMEM],
        out_specs=(VMEM, VMEM),
        compiler_params=LIMIT,
        name="gram",
    )(in_vmem(terms))


def basis_kernel(core_ref, mixed_ref, gram_ref, other_ref, out_ref):
    upper, inverse = factor(gram_ref[...] + other_ref[...])
    basis = [dot(inverse, mixed_ref[k : k + RANK], NN, highest) for k in (0, RANK)]
    half = RANK // 2
    rows = jnp.where(core_ref[0] == 0, upper[:half], upper[half:])
    high, middle, low = (piece.astype(f32) for piece in pieces(rows))
    left = jnp.concatenate([high, middle], axis=0)
    right = jnp.concatenate([low, jnp.zeros_like(low)], axis=0)
    block = jnp.concatenate(basis + [left, right], axis=1).astype(bf16)
    for k in range(out_ref.shape[0]):
        out_ref[k] = block


def basis_of(core, mixed, gram, other, copies):
    return pl.pallas_call(
        basis_kernel,
        out_shape=pltpu.VMEM((copies, RANK, 2 * mixed.shape[1] + LANES), bf16),
        in_specs=[SMEM, VMEM, VMEM, VMEM],
        out_specs=VMEM,
        compiler_params=LIMIT,
        name="basis",
    )(core, in_vmem(mixed), in_vmem(gram), in_vmem(other))


def upper_half(block, width):
    half = RANK // 2
    left = block[:, width : width + RANK]
    return left[:half] + left[half:] + block[:half, width + RANK :]


def spread_kernel(far_ref, own_ref, out_ref, work_ref):
    count = own_ref.shape[0]
    groups = out_ref.shape[0] // count
    blocks = RANK // groups
    width = own_ref.shape[2] - LANES
    wide = width // LANES
    tiles = work_ref.shape[0]
    total = jnp.zeros((RANK, RANK), f32)
    for r in range(count):
        block = own_ref[r].astype(f32)
        for q in range(blocks):
            for t in range(wide):
                work_ref[q * wide + t, pl.ds(r, groups, stride=count), :] = block[
                    q * groups : (q + 1) * groups, t * LANES : (t + 1) * LANES
                ]
        upper = upper_half(block, width)
        total = total + dot(upper, upper, TN, highest)
        work_ref[tiles - 2, pl.ds(r, groups, stride=count), :] = jnp.full(
            (groups, LANES), far_ref[r].astype(f32), f32
        )
    work_ref[tiles - 1] = jnp.zeros((groups * count, LANES), f32)
    for p in range(2):
        low_row = 2 * p * groups
        packed = jnp.concatenate(
            [total[low_row : low_row + groups], total[low_row + groups : low_row + 2 * groups]], axis=1
        )
        for k, piece in enumerate(pieces(packed)):
            work_ref[tiles - 1, pl.ds(2 * k + p, groups, stride=count), :] = piece.astype(f32)
    for t in range(tiles):
        out_ref[:, t * LANES : (t + 1) * LANES] = work_ref[t].astype(bf16)


def spread(far, own, groups):
    count, _, width = own.shape
    total = RANK // groups * (width - LANES) + 2 * LANES
    return pl.pallas_call(
        spread_kernel,
        out_shape=pltpu.VMEM((groups * count, total), bf16),
        in_specs=[SMEM, VMEM],
        out_specs=VMEM,
        scratch_shapes=[pltpu.VMEM((total // LANES, groups * count, LANES), f32)],
        compiler_params=LIMIT,
        name="spread",
    )(far, in_vmem(own))


def choose_kernel(count, core_ref, own_ref, other_ref, out_ref):
    clusters, total = own_ref.shape
    body = total - 2 * LANES
    first = core_ref[0] == 0
    wanted = own_ref[:, body : body + LANES].astype(f32)
    column = lax.broadcasted_iota(jnp.int32, (clusters, clusters), 1).astype(f32)
    select = (wanted == column).astype(bf16)
    own = dot(select, own_ref[:, :body], NN)
    other = dot(select, other_ref[:, :body], NN)
    for t in range(body // LANES):
        mine, others = own[:, t * LANES : (t + 1) * LANES], other[:, t * LANES : (t + 1) * LANES]
        out_ref[:, 2 * t * LANES : (2 * t + 1) * LANES] = jnp.where(first, mine, others).astype(bf16)
        out_ref[:, (2 * t + 1) * LANES : (2 * t + 2) * LANES] = jnp.where(first, others, mine).astype(bf16)
    row = lax.broadcasted_iota(jnp.int32, (count, clusters), 0)
    column = lax.broadcasted_iota(jnp.int32, (count, clusters), 1) % count
    gather = (((column == row) | (column == row + 2) | (column == row + 4)) & (row < 2)).astype(bf16)
    sums = (dot(gather, own_ref[:, body + LANES :], NN) + dot(gather, other_ref[:, body + LANES :], NN))[:2]
    block = jnp.concatenate([piece.astype(f32) for piece in pieces(sums)] + [jnp.zeros((count - 6, LANES), f32)], axis=0)
    out_ref[:, 2 * body :] = jnp.concatenate([block] * (clusters // count), axis=0).astype(bf16)


def choose(core, own, other, count):
    rows, total = own.shape
    return pl.pallas_call(
        functools.partial(choose_kernel, count),
        out_shape=pltpu.VMEM((rows, 2 * (total - 2 * LANES) + LANES), bf16),
        in_specs=[SMEM, VMEM, VMEM],
        out_specs=VMEM,
        compiler_params=LIMIT,
        name="choose",
    )(core, in_vmem(own), in_vmem(other))


def project_kernel(core_ref, own_ref, other_ref, far_ref, out_ref, upper_ref):
    count = own_ref.shape[0]
    first = core_ref[0] == 0
    half = own_ref.shape[2] - LANES
    for i in range(count):
        mine, others = own_ref[i].astype(f32), other_ref[i].astype(f32)
        sides = (jnp.where(first, mine, others), jnp.where(first, others, mine))
        basis = [side[:, t : t + LANES] for t in range(0, half, LANES) for side in sides]
        image = dot(jnp.concatenate(basis, axis=1).astype(bf16), far_ref[i, 0], NN)
        out_ref[i] = jnp.concatenate(pieces(image), axis=0)
        upper_ref[i] = jnp.concatenate([upper_half(side, half) for side in sides], axis=0)


def project(core, own, other, far_tiles):
    count, _, rows, width = far_tiles.shape
    return pl.pallas_call(
        project_kernel,
        out_shape=(
            pltpu.VMEM((count, 3 * RANK, width), bf16),
            pltpu.VMEM((count, RANK, RANK), f32),
        ),
        in_specs=[SMEM] + [VMEM] * 3,
        out_specs=(VMEM, VMEM),
        cost_estimate=pl.CostEstimate(
            flops=2 * count * rows * width * RANK,
            bytes_accessed=count * rows * width * 4,
            transcendentals=0,
        ),
        compiler_params=LIMIT,
        name="project",
    )(core, *[in_vmem(x) for x in (own, other, far_tiles)])


def couple_kernel(scale, image_ref, upper_ref, received_ref, coupling_ref, root_ref, work_ref):
    count = image_ref.shape[0]
    rows, total = received_ref.shape
    groups = rows // count
    blocks = RANK // groups
    wide = (total - LANES) // blocks // LANES
    tiles = work_ref.shape[0]
    for t in range(tiles):
        work_ref[t] = received_ref[:, t * LANES : (t + 1) * LANES].astype(f32)
    parts = []
    for p in range(2):
        packed = sum(work_ref[tiles - 1, pl.ds(2 * k + p, groups, stride=count), :] for k in range(3))
        parts += [packed[:, :RANK], packed[:, RANK:]]
    _, inverse = factor(jnp.concatenate(parts, axis=0))
    for i in range(count):
        far = [
            jnp.concatenate(
                [work_ref[q * wide + t, pl.ds(i, groups, stride=count), :] for t in range(wide)], axis=1
            )
            for q in range(blocks)
        ]
        terms = dot(image_ref[i], jnp.concatenate(far, axis=0).astype(bf16), NT)
        coupling_ref[i, 0] = terms[:RANK] + terms[RANK : 2 * RANK] + terms[2 * RANK :]
    for i in range(count):
        root_ref[i] = dot(upper_ref[i], inverse, NT, highest) * scale


def couple(image, upper, received, scale):
    count = image.shape[0]
    return pl.pallas_call(
        functools.partial(couple_kernel, scale),
        out_shape=(
            jax.ShapeDtypeStruct((count, 1, RANK, RANK), f32),
            jax.ShapeDtypeStruct((count, RANK, RANK), f32),
        ),
        in_specs=[VMEM] * 3,
        out_specs=(VMEM, VMEM),
        scratch_shapes=[pltpu.VMEM((received.shape[1] // LANES, received.shape[0], LANES), f32)],
        compiler_params=LIMIT,
        name="couple",
    )(*[in_vmem(x) for x in (image, upper, received)])


def shards(near_tiles, near_cols, near_count, probes, mixing, far_tiles, far_cols):
    count = probes.shape[0]
    subtrees = lax.axis_size("leaf")
    members = lax.axis_size("blk")
    leaf_pos = lax.axis_index("leaf")
    blk_pos = lax.axis_index("blk")
    core = blk_pos % 2
    pair = [(i, i ^ 1) for i in range(members)]
    lanes = [list(range(c, members, 2)) for c in range(2)]
    shift = [
        (g * members + b, (g + step) * members + b)
        for g in range(subtrees)
        for b in range(members)
        for step in [1 - 2 * (b % 2)]
        if 0 <= g + step < subtrees
    ]

    core = core.reshape(1).astype(jnp.int32)
    live = (blk_pos < near_count).astype(jnp.int32)
    near_meta = jnp.concatenate([near_cols[:, 0] - (leaf_pos * count - REACH), live, core])

    mixing, probes = (pltpu.with_memory_space_constraint(x, pltpu.HBM) for x in (mixing.T, probes))
    part = count // 2
    own = [mixed_probes(start, part, mixing, probes) for start in (0, part)]
    moved = [lax.ppermute(x, ("leaf", "blk"), shift) for x in own]
    other = [lax.ppermute(x, "blk", pair) for x in moved]
    (near_tiles,) = load(own[1], near_tiles)
    keep, send = compress(near_meta, own + moved + other, near_tiles)
    halves = keep + lax.ppermute(send, "blk", pair)
    terms = lax.all_to_all(halves, "blk", 0, 0, tiled=True, axis_index_groups=lanes)
    mixed, gram = gram_of(terms)
    own = basis_of(core, mixed, gram, lax.ppermute(gram, "blk", pair), count)
    own = lax.all_to_all(own, "blk", 0, 0, tiled=True, axis_index_groups=lanes)
    other = lax.ppermute(own, "blk", pair)
    payload = spread(far_cols[:, 0], own, subtrees)
    slices = lax.all_to_all(payload.reshape(subtrees, count, -1), "leaf", 0, 0, tiled=True)
    slices = slices.reshape(payload.shape)
    image, upper = project(core, own, other, far_tiles)
    chosen = choose(core, slices, lax.ppermute(slices, "blk", pair), count)
    received = lax.all_to_all(chosen.reshape(subtrees, count, -1), "leaf", 0, 0, tiled=True)
    scale = math.sqrt(subtrees * count * RANK)
    return couple(image, upper, received.reshape(chosen.shape), scale)


def solution(mesh):
    in_specs = (
        P("leaf", "blk", None, None),
        P("leaf", "blk"),
        P("leaf"),
        P("leaf", None, None),
        P(),
        P("leaf", "blk", None, None),
        P("leaf", "blk"),
    )
    out_specs = (P("leaf", "blk", None, None), P("leaf", None, None))
    return jax.shard_map(shards, mesh=mesh, in_specs=in_specs, out_specs=out_specs, check_vma=False)
```

```python
import functools
import math

import jax
import jax.numpy as jnp
from jax import lax
from jax.experimental import pallas as pl
from jax.experimental.pallas import tpu as pltpu
from jax.sharding import PartitionSpec as P

RANK = 64
REACH = 8
LANES = 128
PANEL = 8

f32 = jnp.float32
bf16 = jnp.bfloat16
highest = lax.Precision.HIGHEST

HBM = pl.BlockSpec(memory_space=pltpu.HBM)
SMEM = pl.BlockSpec(memory_space=pltpu.SMEM)
VMEM = pl.BlockSpec(memory_space=pltpu.VMEM)

LIMIT = pltpu.CompilerParams(vmem_limit_bytes=24 << 20)

NN = (((1,), (0,)), ((), ()))
NT = (((1,), (1,)), ((), ()))
TN = (((0,), (0,)), ((), ()))


def dot(a, b, dims, precision=None):
    return lax.dot_general(a, b, dims, precision=precision, preferred_element_type=f32)


def pieces(x):
    high = x.astype(bf16)
    rest = x - high.astype(f32)
    middle = rest.astype(bf16)
    low = (rest - middle.astype(f32)).astype(bf16)
    return high, middle, low


def in_vmem(x):
    return pltpu.with_memory_space_constraint(x, pltpu.VMEM)


def factor(gram):
    n = gram.shape[0]
    row = lax.broadcasted_iota(jnp.int32, (n, n), 0)
    col = lax.broadcasted_iota(jnp.int32, (n, n), 1)
    tall = lax.broadcasted_iota(jnp.int32, (PANEL, 2 * n), 0)
    work = jnp.concatenate([gram, (row == col).astype(f32)], axis=1)
    panels = [work[k : k + PANEL] for k in range(0, n, PANEL)]
    for k in range(len(panels)):
        columns = [
            [
                jnp.broadcast_to(panels[t][:, k * PANEL + j : k * PANEL + j + 1], (PANEL, 2 * n))
                for j in range(PANEL)
            ]
            for t in range(k, len(panels))
        ]
        scales = jnp.zeros((PANEL, 2 * n), f32)
        for j in range(PANEL):
            inverse = 1.0 / columns[0][j][j : j + 1]
            scales = jnp.where(tall == j, inverse, scales)
            entries = [columns[0][i][j : j + 1] for i in range(PANEL)]
            pivot_row = panels[k][j : j + 1]
            for t in range(k, len(panels)):
                multiplier = columns[t - k][j] * inverse
                if t == k:
                    if j == PANEL - 1:
                        continue
                    multiplier = jnp.where(tall > j, multiplier, 0.0)
                for i in range(j + 1, PANEL):
                    columns[t - k][i] = columns[t - k][i] - multiplier * entries[i]
                panels[t] = panels[t] - multiplier * pivot_row
        panels[k] = panels[k] * jnp.sqrt(scales)
    work = jnp.concatenate(panels, axis=0)
    upper = jnp.where(col >= row, work[:, :n], 0.0)
    return upper, work[:, n:]


def doubled(terms):
    return terms + pltpu.roll(terms, RANK, 1)


def mixed_probes_kernel(start, mixing_hbm, probes_ref, out_ref, mixing_ref, tiles_ref, sems):
    part = out_ref.shape[0]
    first = pltpu.make_async_copy(mixing_hbm, mixing_ref, sems.at[part])
    copies = [pltpu.make_async_copy(probes_ref.at[start + i], tiles_ref.at[i], sems.at[i]) for i in range(part)]
    for copy in [first] + copies:
        copy.start()
    first.wait()
    high, middle, low = pieces(mixing_ref[...])
    weights = jnp.concatenate([piece.astype(f32) for piece in (high, middle, low, low)], axis=0).T.astype(bf16)
    for i, copy in enumerate(copies):
        copy.wait()
        terms = dot(tiles_ref[i], weights, NN)
        mixed = doubled(terms[:, :LANES]) + terms[:, LANES:]
        lane = lax.broadcasted_iota(jnp.int32, mixed.shape, 1)
        high = mixed.astype(bf16).astype(f32)
        out_ref[i] = jnp.where(lane < RANK, high, mixed - high).astype(bf16)


def mixed_probes(start, part, mixing, probes):
    _, rows, width = probes.shape
    return pl.pallas_call(
        functools.partial(mixed_probes_kernel, start),
        out_shape=pltpu.VMEM((part, rows, LANES), bf16),
        in_specs=[HBM, HBM],
        out_specs=VMEM,
        scratch_shapes=[
            pltpu.VMEM(mixing.shape, f32),
            pltpu.VMEM((part, rows, width), bf16),
            pltpu.SemaphoreType.DMA((part + 1,)),
        ],
        cost_estimate=pl.CostEstimate(
            flops=2 * part * rows * width * 3 * RANK,
            bytes_accessed=part * rows * (2 * width + 4 * RANK),
            transcendentals=0,
        ),
        compiler_params=LIMIT,
        name="mixed_probes",
    )(mixing, probes)


def sketch_kernel(
    meta_ref, own_a, own_b, moved_a, moved_b, other_a, other_b, near_ref, keep_ref, send_ref,
    pick_ref, tiles_ref, sems
):
    count = near_ref.shape[0]
    part = own_a.shape[0]
    core = meta_ref[2 * count]
    copies = [pltpu.make_async_copy(near_ref.at[i, 0], tiles_ref.at[i], sems.at[i]) for i in range(count)]
    for copy in copies:
        copy.start()
    sources = (
        (own_a, 2), (own_b, 3), (moved_a, 4 * core), (moved_b, 4 * core + 1),
        (other_a, 4 - 4 * core), (other_b, 5 - 4 * core),
    )

    def pick(i):
        column = jnp.clip(meta_ref[i], 0, 6 * part - 1)
        for source, group in sources:

            @pl.when(column // part == group)
            def _():
                pick_ref[i] = source[column % part]

    for i in range(count):
        pick(i)
    for i, copy in enumerate(copies):
        copy.wait()
        mixed = doubled(dot(tiles_ref[i], pick_ref[i], NN))
        rows = mixed.shape[0] // 4
        lane = lax.broadcasted_iota(jnp.int32, (rows, LANES), 1)
        live = meta_ref[count + i] > 0
        quarters = [jnp.where(live, mixed[k * rows : (k + 1) * rows], 0.0) for k in range(4)]
        left = jnp.where(lane < RANK, quarters[0], quarters[2])
        right = jnp.where(lane < RANK, quarters[1], quarters[3])
        keep_ref[i] = jnp.where(core == 0, left, right)
        send_ref[i] = jnp.where(core == 0, right, left)


def compress(meta, parts, near_tiles):
    count, _, rows, width = near_tiles.shape
    shape = pltpu.VMEM((count, rows // 4, LANES), f32)
    near_tiles = pltpu.with_memory_space_constraint(near_tiles, pltpu.HBM)
    return pl.pallas_call(
        sketch_kernel,
        out_shape=(shape, shape),
        in_specs=[SMEM] + [VMEM] * 6 + [HBM],
        out_specs=(VMEM, VMEM),
        scratch_shapes=[
            pltpu.VMEM((count, rows, LANES), bf16),
            pltpu.VMEM((count, rows, width), bf16),
            pltpu.SemaphoreType.DMA((count,)),
        ],
        cost_estimate=pl.CostEstimate(
            flops=2 * count * rows * width * LANES,
            bytes_accessed=count * rows * (2 * width + 16 * RANK),
            transcendentals=0,
        ),
        compiler_params=LIMIT,
        name="compress",
    )(meta, *[in_vmem(part) for part in parts], near_tiles)


def gram_kernel(terms_ref, mixed_ref, gram_ref):
    total = terms_ref[0]
    for k in range(1, terms_ref.shape[0]):
        total = total + terms_ref[k]
    mixed = total.T
    mixed_ref[...] = mixed
    first, second = mixed[:RANK], mixed[RANK:]
    gram_ref[...] = dot(first, first, NT, highest) + dot(second, second, NT, highest)


def gram_of(terms):
    return pl.pallas_call(
        gram_kernel,
        out_shape=(
            pltpu.VMEM((terms.shape[2], terms.shape[1]), f32),
            pltpu.VMEM((RANK, RANK), f32),
        ),
        in_specs=[VMEM],
        out_specs=(VMEM, VMEM),
        compiler_params=LIMIT,
        name="gram",
    )(in_vmem(terms))


def basis_kernel(core_ref, mixed_ref, gram_ref, other_ref, out_ref):
    upper, inverse = factor(gram_ref[...] + other_ref[...])
    basis = [dot(inverse, mixed_ref[k : k + RANK], NN, highest) for k in (0, RANK)]
    half = RANK // 2
    rows = jnp.where(core_ref[0] == 0, upper[:half], upper[half:])
    high, middle, low = (piece.astype(f32) for piece in pieces(rows))
    left = jnp.concatenate([high, middle], axis=0)
    right = jnp.concatenate([low, jnp.zeros_like(low)], axis=0)
    block = jnp.concatenate(basis + [left, right], axis=1).astype(bf16)
    for k in range(out_ref.shape[0]):
        out_ref[k] = block


def basis_of(core, mixed, gram, other, copies):
    return pl.pallas_call(
        basis_kernel,
        out_shape=pltpu.VMEM((copies, RANK, 2 * mixed.shape[1] + LANES), bf16),
        in_specs=[SMEM, VMEM, VMEM, VMEM],
        out_specs=VMEM,
        compiler_params=LIMIT,
        name="basis",
    )(core, in_vmem(mixed), in_vmem(gram), in_vmem(other))


def upper_half(block, width):
    half = RANK // 2
    left = block[:, width : width + RANK]
    return left[:half] + left[half:] + block[:half, width + RANK :]


def spread_kernel(far_ref, own_ref, out_ref, work_ref):
    count = own_ref.shape[0]
    groups = out_ref.shape[0] // count
    blocks = RANK // groups
    width = own_ref.shape[2] - LANES
    wide = width // LANES
    tiles = work_ref.shape[0]
    total = jnp.zeros((RANK, RANK), f32)
    for r in range(count):
        block = own_ref[r].astype(f32)
        for q in range(blocks):
            for t in range(wide):
                work_ref[q * wide + t, pl.ds(r, groups, stride=count), :] = block[
                    q * groups : (q + 1) * groups, t * LANES : (t + 1) * LANES
                ]
        upper = upper_half(block, width)
        total = total + dot(upper, upper, TN, highest)
        work_ref[tiles - 2, pl.ds(r, groups, stride=count), :] = jnp.full(
            (groups, LANES), far_ref[r].astype(f32), f32
        )
    work_ref[tiles - 1] = jnp.zeros((groups * count, LANES), f32)
    for p in range(2):
        low_row = 2 * p * groups
        packed = jnp.concatenate(
            [total[low_row : low_row + groups], total[low_row + groups : low_row + 2 * groups]], axis=1
        )
        for k, piece in enumerate(pieces(packed)):
            work_ref[tiles - 1, pl.ds(2 * k + p, groups, stride=count), :] = piece.astype(f32)
    for t in range(tiles):
        out_ref[:, t * LANES : (t + 1) * LANES] = work_ref[t].astype(bf16)


def spread(far, own, groups):
    count, _, width = own.shape
    total = RANK // groups * (width - LANES) + 2 * LANES
    return pl.pallas_call(
        spread_kernel,
        out_shape=pltpu.VMEM((groups * count, total), bf16),
        in_specs=[SMEM, VMEM],
        out_specs=VMEM,
        scratch_shapes=[pltpu.VMEM((total // LANES, groups * count, LANES), f32)],
        compiler_params=LIMIT,
        name="spread",
    )(far, in_vmem(own))


def choose_kernel(count, core_ref, own_ref, other_ref, out_ref):
    clusters, total = own_ref.shape
    body = total - 2 * LANES
    first = core_ref[0] == 0
    wanted = own_ref[:, body : body + LANES].astype(f32)
    column = lax.broadcasted_iota(jnp.int32, (clusters, clusters), 1).astype(f32)
    select = (wanted == column).astype(bf16)
    own = dot(select, own_ref[:, :body], NN)
    other = dot(select, other_ref[:, :body], NN)
    for t in range(body // LANES):
        mine, others = own[:, t * LANES : (t + 1) * LANES], other[:, t * LANES : (t + 1) * LANES]
        out_ref[:, 2 * t * LANES : (2 * t + 1) * LANES] = jnp.where(first, mine, others).astype(bf16)
        out_ref[:, (2 * t + 1) * LANES : (2 * t + 2) * LANES] = jnp.where(first, others, mine).astype(bf16)
    row = lax.broadcasted_iota(jnp.int32, (count, clusters), 0)
    column = lax.broadcasted_iota(jnp.int32, (count, clusters), 1) % count
    gather = (((column == row) | (column == row + 2) | (column == row + 4)) & (row < 2)).astype(bf16)
    sums = (dot(gather, own_ref[:, body + LANES :], NN) + dot(gather, other_ref[:, body + LANES :], NN))[:2]
    block = jnp.concatenate([piece.astype(f32) for piece in pieces(sums)] + [jnp.zeros((count - 6, LANES), f32)], axis=0)
    out_ref[:, 2 * body :] = jnp.concatenate([block] * (clusters // count), axis=0).astype(bf16)


def choose(core, own, other, count):
    rows, total = own.shape
    return pl.pallas_call(
        functools.partial(choose_kernel, count),
        out_shape=pltpu.VMEM((rows, 2 * (total - 2 * LANES) + LANES), bf16),
        in_specs=[SMEM, VMEM, VMEM],
        out_specs=VMEM,
        compiler_params=LIMIT,
        name="choose",
    )(core, in_vmem(own), in_vmem(other))


def project_kernel(core_ref, own_ref, other_ref, far_ref, out_ref, upper_ref):
    count = own_ref.shape[0]
    first = core_ref[0] == 0
    half = own_ref.shape[2] - LANES
    for i in range(count):
        mine, others = own_ref[i].astype(f32), other_ref[i].astype(f32)
        sides = (jnp.where(first, mine, others), jnp.where(first, others, mine))
        basis = [side[:, t : t + LANES] for t in range(0, half, LANES) for side in sides]
        image = dot(jnp.concatenate(basis, axis=1).astype(bf16), far_ref[i, 0], NN)
        out_ref[i] = jnp.concatenate(pieces(image), axis=0)
        upper_ref[i] = jnp.concatenate([upper_half(side, half) for side in sides], axis=0)


def project(core, own, other, far_tiles):
    count, _, rows, width = far_tiles.shape
    return pl.pallas_call(
        project_kernel,
        out_shape=(
            pltpu.VMEM((count, 3 * RANK, width), bf16),
            pltpu.VMEM((count, RANK, RANK), f32),
        ),
        in_specs=[SMEM] + [VMEM] * 3,
        out_specs=(VMEM, VMEM),
        cost_estimate=pl.CostEstimate(
            flops=2 * count * rows * width * RANK,
            bytes_accessed=count * rows * width * 4,
            transcendentals=0,
        ),
        compiler_params=LIMIT,
        name="project",
    )(core, *[in_vmem(x) for x in (own, other, far_tiles)])


def couple_kernel(scale, image_ref, upper_ref, received_ref, coupling_ref, root_ref, work_ref):
    count = image_ref.shape[0]
    rows, total = received_ref.shape
    groups = rows // count
    blocks = RANK // groups
    wide = (total - LANES) // blocks // LANES
    tiles = work_ref.shape[0]
    for t in range(tiles):
        work_ref[t] = received_ref[:, t * LANES : (t + 1) * LANES].astype(f32)
    parts = []
    for p in range(2):
        packed = sum(work_ref[tiles - 1, pl.ds(2 * k + p, groups, stride=count), :] for k in range(3))
        parts += [packed[:, :RANK], packed[:, RANK:]]
    _, inverse = factor(jnp.concatenate(parts, axis=0))
    for i in range(count):
        far = [
            jnp.concatenate(
                [work_ref[q * wide + t, pl.ds(i, groups, stride=count), :] for t in range(wide)], axis=1
            )
            for q in range(blocks)
        ]
        terms = dot(image_ref[i], jnp.concatenate(far, axis=0).astype(bf16), NT)
        coupling_ref[i, 0] = terms[:RANK] + terms[RANK : 2 * RANK] + terms[2 * RANK :]
    for i in range(count):
        root_ref[i] = dot(upper_ref[i], inverse, NT, highest) * scale


def couple(image, upper, received, scale):
    count = image.shape[0]
    return pl.pallas_call(
        functools.partial(couple_kernel, scale),
        out_shape=(
            jax.ShapeDtypeStruct((count, 1, RANK, RANK), f32),
            jax.ShapeDtypeStruct((count, RANK, RANK), f32),
        ),
        in_specs=[VMEM] * 3,
        out_specs=(VMEM, VMEM),
        scratch_shapes=[pltpu.VMEM((received.shape[1] // LANES, received.shape[0], LANES), f32)],
        compiler_params=LIMIT,
        name="couple",
    )(*[in_vmem(x) for x in (image, upper, received)])


def shards(near_tiles, near_cols, near_count, probes, mixing, far_tiles, far_cols):
    count = probes.shape[0]
    subtrees = lax.axis_size("leaf")
    members = lax.axis_size("blk")
    leaf_pos = lax.axis_index("leaf")
    blk_pos = lax.axis_index("blk")
    core = blk_pos % 2
    pair = [(i, i ^ 1) for i in range(members)]
    lanes = [list(range(c, members, 2)) for c in range(2)]
    shift = [
        (g * members + b, (g + step) * members + b)
        for g in range(subtrees)
        for b in range(members)
        for step in [1 - 2 * (b % 2)]
        if 0 <= g + step < subtrees
    ]

    core = core.reshape(1).astype(jnp.int32)
    live = (blk_pos < near_count).astype(jnp.int32)
    near_meta = jnp.concatenate([near_cols[:, 0] - (leaf_pos * count - REACH), live, core])

    mixing, probes = (pltpu.with_memory_space_constraint(x, pltpu.HBM) for x in (mixing.T, probes))
    part = count // 2
    own = [mixed_probes(start, part, mixing, probes) for start in (0, part)]
    moved = [lax.ppermute(x, ("leaf", "blk"), shift) for x in own]
    other = [lax.ppermute(x, "blk", pair) for x in moved]
    keep, send = compress(near_meta, own + moved + other, near_tiles)
    halves = keep + lax.ppermute(send, "blk", pair)
    terms = lax.all_to_all(halves, "blk", 0, 0, tiled=True, axis_index_groups=lanes)
    mixed, gram = gram_of(terms)
    own = basis_of(core, mixed, gram, lax.ppermute(gram, "blk", pair), count)
    own = lax.all_to_all(own, "blk", 0, 0, tiled=True, axis_index_groups=lanes)
    other = lax.ppermute(own, "blk", pair)
    payload = spread(far_cols[:, 0], own, subtrees)
    slices = lax.all_to_all(payload.reshape(subtrees, count, -1), "leaf", 0, 0, tiled=True)
    slices = slices.reshape(payload.shape)
    image, upper = project(core, own, other, far_tiles)
    chosen = choose(core, slices, lax.ppermute(slices, "blk", pair), count)
    received = lax.all_to_all(chosen.reshape(subtrees, count, -1), "leaf", 0, 0, tiled=True)
    scale = math.sqrt(subtrees * count * RANK)
    return couple(image, upper, received.reshape(chosen.shape), scale)


def solution(mesh):
    in_specs = (
        P("leaf", "blk", None, None),
        P("leaf", "blk"),
        P("leaf"),
        P("leaf", None, None),
        P(),
        P("leaf", "blk", None, None),
        P("leaf", "blk"),
    )
    out_specs = (P("leaf", "blk", None, None), P("leaf", None, None))
    return jax.shard_map(shards, mesh=mesh, in_specs=in_specs, out_specs=out_specs, check_vma=False)
```

```python
import functools
import math

import jax
import jax.numpy as jnp
from jax import lax
from jax.experimental import pallas as pl
from jax.experimental.pallas import tpu as pltpu
from jax.sharding import PartitionSpec as P

RANK = 64
REACH = 8
LANES = 128
PANEL = 8

f32 = jnp.float32
bf16 = jnp.bfloat16
highest = lax.Precision.HIGHEST

HBM = pl.BlockSpec(memory_space=pltpu.HBM)
SMEM = pl.BlockSpec(memory_space=pltpu.SMEM)
VMEM = pl.BlockSpec(memory_space=pltpu.VMEM)

LIMIT = pltpu.CompilerParams(vmem_limit_bytes=24 << 20)

NN = (((1,), (0,)), ((), ()))
NT = (((1,), (1,)), ((), ()))
TN = (((0,), (0,)), ((), ()))


def dot(a, b, dims, precision=None):
    return lax.dot_general(a, b, dims, precision=precision, preferred_element_type=f32)


def pieces(x):
    high = x.astype(bf16)
    rest = x - high.astype(f32)
    middle = rest.astype(bf16)
    low = (rest - middle.astype(f32)).astype(bf16)
    return high, middle, low


def in_vmem(x):
    return pltpu.with_memory_space_constraint(x, pltpu.VMEM)


def factor(gram, beside=lambda k: None):
    n = gram.shape[0]
    row = lax.broadcasted_iota(jnp.int32, (n, n), 0)
    col = lax.broadcasted_iota(jnp.int32, (n, n), 1)
    tall = lax.broadcasted_iota(jnp.int32, (PANEL, 2 * n), 0)
    work = jnp.concatenate([gram, (row == col).astype(f32)], axis=1)
    panels = [work[k : k + PANEL] for k in range(0, n, PANEL)]
    for k in range(len(panels)):
        columns = [
            [
                jnp.broadcast_to(panels[t][:, k * PANEL + j : k * PANEL + j + 1], (PANEL, 2 * n))
                for j in range(PANEL)
            ]
            for t in range(k, len(panels))
        ]
        scales = jnp.zeros((PANEL, 2 * n), f32)
        for j in range(PANEL):
            inverse = 1.0 / columns[0][j][j : j + 1]
            scales = jnp.where(tall == j, inverse, scales)
            entries = [columns[0][i][j : j + 1] for i in range(PANEL)]
            pivot_row = panels[k][j : j + 1]
            for t in range(k, len(panels)):
                multiplier = columns[t - k][j] * inverse
                if t == k:
                    if j == PANEL - 1:
                        continue
                    multiplier = jnp.where(tall > j, multiplier, 0.0)
                for i in range(j + 1, PANEL):
                    columns[t - k][i] = columns[t - k][i] - multiplier * entries[i]
                panels[t] = panels[t] - multiplier * pivot_row
            if j == PANEL // 2:
                beside(k)
        panels[k] = panels[k] * jnp.sqrt(scales)
    work = jnp.concatenate(panels, axis=0)
    upper = jnp.where(col >= row, work[:, :n], 0.0)
    return upper, work[:, n:]


def weights_of(x):
    high, middle, low = (piece.astype(f32) for piece in pieces(x))
    lane = lax.broadcasted_iota(jnp.int32, x.shape, 1)
    return jnp.concatenate([jnp.where(lane < RANK, high, middle), low], axis=1).astype(bf16)


def weighted(x, weights):
    terms = dot(x, weights, NN)
    first, last = terms[:, :LANES], terms[:, LANES:]
    return first + pltpu.roll(first, RANK, 1) + last


def folded(x):
    rows = x.shape[0] // 2
    lane = lax.broadcasted_iota(jnp.int32, (rows, LANES), 1)
    return jnp.where(lane < RANK, x[:rows], x[rows:])


def unfolded(x):
    lane = lax.broadcasted_iota(jnp.int32, x.shape, 1)
    turned = pltpu.roll(x, RANK, 1)
    return jnp.concatenate([jnp.where(lane < RANK, x, turned), jnp.where(lane < RANK, turned, x)], axis=0)


def mixed_probes_kernel(start, mixing_hbm, probes_ref, out_ref, mixing_ref, tiles_ref, sems):
    part = out_ref.shape[0]
    first = pltpu.make_async_copy(mixing_hbm, mixing_ref, sems.at[part])
    copies = [pltpu.make_async_copy(probes_ref.at[start + i], tiles_ref.at[i], sems.at[i]) for i in range(part)]
    for copy in [first] + copies[:2]:
        copy.start()
    first.wait()
    mixing = mixing_ref[...]
    weights = weights_of(jnp.concatenate([mixing, mixing], axis=0).T)
    for i, copy in enumerate(copies):
        copy.wait()
        if i + 2 < part:
            copies[i + 2].start()
        out_ref[i] = folded(weighted(tiles_ref[i], weights))


def mixed_probes(start, part, mixing, probes):
    _, rows, width = probes.shape
    return pl.pallas_call(
        functools.partial(mixed_probes_kernel, start),
        out_shape=pltpu.VMEM((part, rows // 2, LANES), f32),
        in_specs=[HBM, HBM],
        out_specs=VMEM,
        scratch_shapes=[
            pltpu.VMEM(mixing.shape, f32),
            pltpu.VMEM((part, rows, width), bf16),
            pltpu.SemaphoreType.DMA((part + 1,)),
        ],
        cost_estimate=pl.CostEstimate(
            flops=2 * part * rows * width * 3 * RANK,
            bytes_accessed=part * rows * (2 * width + 4 * RANK),
            transcendentals=0,
        ),
        compiler_params=LIMIT,
        name="mixed_probes",
    )(mixing, probes)


def load_kernel(meta_ref, after_ref, tiles_ref, out_ref, sems):
    del meta_ref, after_ref
    part = out_ref.shape[0]
    copies = [pltpu.make_async_copy(tiles_ref.at[i, 0], out_ref.at[i], sems.at[i]) for i in range(part)]
    for copy in copies:
        copy.start()
    for copy in copies:
        copy.wait()


def load(meta, after, tiles, part):
    _, _, rows, width = tiles.shape
    return pl.pallas_call(
        load_kernel,
        out_shape=pltpu.VMEM((part, rows, width), tiles.dtype),
        in_specs=[SMEM, VMEM, HBM],
        out_specs=VMEM,
        scratch_shapes=[pltpu.SemaphoreType.DMA((part,))],
        cost_estimate=pl.CostEstimate(
            flops=0, bytes_accessed=4 * part * rows * width, transcendentals=0
        ),
        compiler_params=LIMIT,
        name="load",
    )(meta, in_vmem(after), tiles)


def sketch_kernel(
    meta_ref, own_a, own_b, moved_a, moved_b, other_a, other_b, ready_ref, near_ref, keep_ref, send_ref,
    pick_ref, tiles_ref, sems
):
    count = near_ref.shape[0]
    ready = ready_ref.shape[0]
    copies = [
        pltpu.make_async_copy(near_ref.at[ready + i, 0], tiles_ref.at[i], sems.at[i]) for i in range(count - ready)
    ]
    for copy in copies:
        copy.start()
    part = own_a.shape[0]
    core = meta_ref[2 * count]
    sources = (
        (own_a, 2), (own_b, 3), (moved_a, 4 * core), (moved_b, 4 * core + 1),
        (other_a, 4 - 4 * core), (other_b, 5 - 4 * core),
    )

    def pick(i):
        column = jnp.clip(meta_ref[i], 0, 6 * part - 1)
        for source, group in sources:

            @pl.when(column // part == group)
            def _():
                pick_ref[i] = source[column % part]

    for i in range(count):
        pick(i)
    for i in range(count):
        if i >= ready:
            copies[i - ready].wait()
        tile = ready_ref[i] if i < ready else tiles_ref[i - ready]
        mixed = folded(weighted(tile, weights_of(unfolded(pick_ref[i]))))
        mixed = jnp.where(meta_ref[count + i] > 0, mixed, 0.0)
        rows = mixed.shape[0] // 2
        keep_ref[i] = jnp.where(core == 0, mixed[:rows], mixed[rows:])
        send_ref[i] = jnp.where(core == 0, mixed[rows:], mixed[:rows])


def compress(meta, parts, ready, near_tiles):
    count, _, rows, width = near_tiles.shape
    shape = pltpu.VMEM((count, rows // 4, LANES), f32)
    return pl.pallas_call(
        sketch_kernel,
        out_shape=(shape, shape),
        in_specs=[SMEM] + [VMEM] * 7 + [HBM],
        out_specs=(VMEM, VMEM),
        scratch_shapes=[
            pltpu.VMEM((count, rows // 2, LANES), f32),
            pltpu.VMEM((count - ready.shape[0], rows, width), bf16),
            pltpu.SemaphoreType.DMA((count - ready.shape[0],)),
        ],
        cost_estimate=pl.CostEstimate(
            flops=2 * count * rows * width * 3 * RANK,
            bytes_accessed=count * rows * (2 * width + 16 * RANK),
            transcendentals=0,
        ),
        compiler_params=LIMIT,
        name="compress",
    )(meta, *[in_vmem(x) for x in (*parts, ready)], near_tiles)


def gram_kernel(terms_ref, mixed_ref, gram_ref):
    total = terms_ref[0]
    for k in range(1, terms_ref.shape[0]):
        total = total + terms_ref[k]
    mixed = total.T
    mixed_ref[...] = mixed
    first, second = mixed[:RANK], mixed[RANK:]
    gram_ref[...] = dot(first, first, NT, highest) + dot(second, second, NT, highest)


def gram_of(terms):
    return pl.pallas_call(
        gram_kernel,
        out_shape=(
            pltpu.VMEM((terms.shape[2], terms.shape[1]), f32),
            pltpu.VMEM((RANK, RANK), f32),
        ),
        in_specs=[VMEM],
        out_specs=(VMEM, VMEM),
        compiler_params=LIMIT,
        name="gram",
    )(in_vmem(terms))


def basis_kernel(core_ref, mixed_ref, gram_ref, other_ref, out_ref):
    upper, inverse = factor(gram_ref[...] + other_ref[...])
    basis = [dot(inverse, mixed_ref[k : k + RANK], NN, highest) for k in (0, RANK)]
    half = RANK // 2
    rows = jnp.where(core_ref[0] == 0, upper[:half], upper[half:])
    high, middle, low = (piece.astype(f32) for piece in pieces(rows))
    left = jnp.concatenate([high, middle], axis=0)
    right = jnp.concatenate([low, jnp.zeros_like(low)], axis=0)
    block = jnp.concatenate(basis + [left, right], axis=1).astype(bf16)
    for k in range(out_ref.shape[0]):
        out_ref[k] = block


def basis_of(core, mixed, gram, other, copies):
    return pl.pallas_call(
        basis_kernel,
        out_shape=pltpu.VMEM((copies, RANK, 2 * mixed.shape[1] + LANES), bf16),
        in_specs=[SMEM, VMEM, VMEM, VMEM],
        out_specs=VMEM,
        compiler_params=LIMIT,
        name="basis",
    )(core, in_vmem(mixed), in_vmem(gram), in_vmem(other))


def upper_half(block, width):
    half = RANK // 2
    left = block[:, width : width + RANK]
    return left[:half] + left[half:] + block[:half, width + RANK :]


def spread_kernel(far_ref, own_ref, out_ref, work_ref):
    count = own_ref.shape[0]
    groups = out_ref.shape[0] // count
    blocks = RANK // groups
    width = own_ref.shape[2] - LANES
    wide = width // LANES
    tiles = work_ref.shape[0]
    total = jnp.zeros((RANK, RANK), f32)
    for r in range(count):
        block = own_ref[r].astype(f32)
        for q in range(blocks):
            for t in range(wide):
                work_ref[q * wide + t, pl.ds(r, groups, stride=count), :] = block[
                    q * groups : (q + 1) * groups, t * LANES : (t + 1) * LANES
                ]
        upper = upper_half(block, width)
        total = total + dot(upper, upper, TN, highest)
        work_ref[tiles - 2, pl.ds(r, groups, stride=count), :] = jnp.full(
            (groups, LANES), far_ref[r].astype(f32), f32
        )
    work_ref[tiles - 1] = jnp.zeros((groups * count, LANES), f32)
    for p in range(2):
        low_row = 2 * p * groups
        packed = jnp.concatenate(
            [total[low_row : low_row + groups], total[low_row + groups : low_row + 2 * groups]], axis=1
        )
        for k, piece in enumerate(pieces(packed)):
            work_ref[tiles - 1, pl.ds(2 * k + p, groups, stride=count), :] = piece.astype(f32)
    for t in range(tiles):
        out_ref[:, t * LANES : (t + 1) * LANES] = work_ref[t].astype(bf16)


def spread(far, own, groups):
    count, _, width = own.shape
    total = RANK // groups * (width - LANES) + 2 * LANES
    return pl.pallas_call(
        spread_kernel,
        out_shape=pltpu.VMEM((groups * count, total), bf16),
        in_specs=[SMEM, VMEM],
        out_specs=VMEM,
        scratch_shapes=[pltpu.VMEM((total // LANES, groups * count, LANES), f32)],
        compiler_params=LIMIT,
        name="spread",
    )(far, in_vmem(own))


def choose_kernel(count, core_ref, own_ref, other_ref, out_ref):
    clusters, total = own_ref.shape
    body = total - 2 * LANES
    first = core_ref[0] == 0
    wanted = own_ref[:, body : body + LANES].astype(f32)
    column = lax.broadcasted_iota(jnp.int32, (clusters, clusters), 1).astype(f32)
    select = (wanted == column).astype(bf16)
    own = dot(select, own_ref[:, :body], NN)
    other = dot(select, other_ref[:, :body], NN)
    for t in range(body // LANES):
        mine, others = own[:, t * LANES : (t + 1) * LANES], other[:, t * LANES : (t + 1) * LANES]
        out_ref[:, 2 * t * LANES : (2 * t + 1) * LANES] = jnp.where(first, mine, others).astype(bf16)
        out_ref[:, (2 * t + 1) * LANES : (2 * t + 2) * LANES] = jnp.where(first, others, mine).astype(bf16)
    row = lax.broadcasted_iota(jnp.int32, (count, clusters), 0)
    column = lax.broadcasted_iota(jnp.int32, (count, clusters), 1) % count
    gather = (((column == row) | (column == row + 2) | (column == row + 4)) & (row < 2)).astype(bf16)
    sums = (dot(gather, own_ref[:, body + LANES :], NN) + dot(gather, other_ref[:, body + LANES :], NN))[:2]
    block = jnp.concatenate([piece.astype(f32) for piece in pieces(sums)] + [jnp.zeros((count - 6, LANES), f32)], axis=0)
    out_ref[:, 2 * body :] = jnp.concatenate([block] * (clusters // count), axis=0).astype(bf16)


def choose(core, own, other, count):
    rows, total = own.shape
    return pl.pallas_call(
        functools.partial(choose_kernel, count),
        out_shape=pltpu.VMEM((rows, 2 * (total - 2 * LANES) + LANES), bf16),
        in_specs=[SMEM, VMEM, VMEM],
        out_specs=VMEM,
        compiler_params=LIMIT,
        name="choose",
    )(core, in_vmem(own), in_vmem(other))


def project_kernel(core_ref, own_ref, other_ref, far_ref, out_ref, upper_ref):
    count = own_ref.shape[0]
    first = core_ref[0] == 0
    half = own_ref.shape[2] - LANES
    for i in range(count):
        mine, others = own_ref[i].astype(f32), other_ref[i].astype(f32)
        sides = (jnp.where(first, mine, others), jnp.where(first, others, mine))
        basis = [side[:, t : t + LANES] for t in range(0, half, LANES) for side in sides]
        image = dot(jnp.concatenate(basis, axis=1).astype(bf16), far_ref[i, 0], NN)
        out_ref[i] = jnp.concatenate(pieces(image), axis=0)
        upper_ref[i] = jnp.concatenate([upper_half(side, half) for side in sides], axis=0)


def project(core, own, other, far_tiles):
    count, _, rows, width = far_tiles.shape
    return pl.pallas_call(
        project_kernel,
        out_shape=(
            pltpu.VMEM((count, 3 * RANK, width), bf16),
            pltpu.VMEM((count, RANK, RANK), f32),
        ),
        in_specs=[SMEM] + [VMEM] * 3,
        out_specs=(VMEM, VMEM),
        cost_estimate=pl.CostEstimate(
            flops=2 * count * rows * width * RANK,
            bytes_accessed=count * rows * width * 4,
            transcendentals=0,
        ),
        compiler_params=LIMIT,
        name="project",
    )(core, *[in_vmem(x) for x in (own, other, far_tiles)])


def couple_kernel(scale, image_ref, upper_ref, received_ref, coupling_ref, root_ref, work_ref):
    count = image_ref.shape[0]
    rows, total = received_ref.shape
    groups = rows // count
    blocks = RANK // groups
    wide = (total - LANES) // blocks // LANES
    tiles = work_ref.shape[0]
    for t in range(tiles):
        work_ref[t] = received_ref[:, t * LANES : (t + 1) * LANES].astype(f32)
    parts = []
    for p in range(2):
        packed = sum(work_ref[tiles - 1, pl.ds(2 * k + p, groups, stride=count), :] for k in range(3))
        parts += [packed[:, :RANK], packed[:, RANK:]]

    def coupling(i):
        far = [
            jnp.concatenate(
                [work_ref[q * wide + t, pl.ds(i, groups, stride=count), :] for t in range(wide)], axis=1
            )
            for q in range(blocks)
        ]
        terms = dot(image_ref[i], jnp.concatenate(far, axis=0).astype(bf16), NT)
        coupling_ref[i, 0] = terms[:RANK] + terms[RANK : 2 * RANK] + terms[2 * RANK :]

    _, inverse = factor(jnp.concatenate(parts, axis=0), coupling)
    for i in range(count):
        root_ref[i] = dot(upper_ref[i], inverse, NT, highest) * scale


def couple(image, upper, received, scale):
    count = image.shape[0]
    return pl.pallas_call(
        functools.partial(couple_kernel, scale),
        out_shape=(
            jax.ShapeDtypeStruct((count, 1, RANK, RANK), f32),
            jax.ShapeDtypeStruct((count, RANK, RANK), f32),
        ),
        in_specs=[VMEM] * 3,
        out_specs=(VMEM, VMEM),
        scratch_shapes=[pltpu.VMEM((received.shape[1] // LANES, received.shape[0], LANES), f32)],
        compiler_params=LIMIT,
        name="couple",
    )(*[in_vmem(x) for x in (image, upper, received)])


def shards(near_tiles, near_cols, near_count, probes, mixing, far_tiles, far_cols):
    count = probes.shape[0]
    subtrees = lax.axis_size("leaf")
    members = lax.axis_size("blk")
    leaf_pos = lax.axis_index("leaf")
    blk_pos = lax.axis_index("blk")
    core = blk_pos % 2
    pair = [(i, i ^ 1) for i in range(members)]
    lanes = [list(range(c, members, 2)) for c in range(2)]
    shift = [
        (g * members + b, (g + step) * members + b)
        for g in range(subtrees)
        for b in range(members)
        for step in [1 - 2 * (b % 2)]
        if 0 <= g + step < subtrees
    ]

    core = core.reshape(1).astype(jnp.int32)
    live = (blk_pos < near_count).astype(jnp.int32)
    near_meta = jnp.concatenate([near_cols[:, 0] - (leaf_pos * count - REACH), live, core])

    mixing, probes = (pltpu.with_memory_space_constraint(x, pltpu.HBM) for x in (mixing.T, probes))
    part = count // 2
    own = [mixed_probes(start, part, mixing, probes) for start in (0, part)]
    moved = [lax.ppermute(x, ("leaf", "blk"), shift) for x in own]
    other = [lax.ppermute(x, "blk", pair) for x in moved]
    near_tiles = pltpu.with_memory_space_constraint(near_tiles, pltpu.HBM)
    ready = load(near_meta, own[1], near_tiles, part)
    keep, send = compress(near_meta, own + moved + other, ready, near_tiles)
    halves = keep + lax.ppermute(send, "blk", pair)
    terms = lax.all_to_all(halves, "blk", 0, 0, tiled=True, axis_index_groups=lanes)
    mixed, gram = gram_of(terms)
    own = basis_of(core, mixed, gram, lax.ppermute(gram, "blk", pair), count)
    own = lax.all_to_all(own, "blk", 0, 0, tiled=True, axis_index_groups=lanes)
    other = lax.ppermute(own, "blk", pair)
    payload = spread(far_cols[:, 0], own, subtrees)
    slices = lax.all_to_all(payload.reshape(subtrees, count, -1), "leaf", 0, 0, tiled=True)
    slices = slices.reshape(payload.shape)
    image, upper = project(core, own, other, far_tiles)
    chosen = choose(core, slices, lax.ppermute(slices, "blk", pair), count)
    received = lax.all_to_all(chosen.reshape(subtrees, count, -1), "leaf", 0, 0, tiled=True)
    scale = math.sqrt(subtrees * count * RANK)
    return couple(image, upper, received.reshape(chosen.shape), scale)


def solution(mesh):
    in_specs = (
        P("leaf", "blk", None, None),
        P("leaf", "blk"),
        P("leaf"),
        P("leaf", None, None),
        P(),
        P("leaf", "blk", None, None),
        P("leaf", "blk"),
    )
    out_specs = (P("leaf", "blk", None, None), P("leaf", None, None))
    return jax.shard_map(shards, mesh=mesh, in_specs=in_specs, out_specs=out_specs, check_vma=False)
```

```python
import functools
import math

import jax
import jax.numpy as jnp
from jax import lax
from jax.experimental import pallas as pl
from jax.experimental.pallas import tpu as pltpu
from jax.sharding import PartitionSpec as P

RANK = 64
REACH = 8
LANES = 128
PANEL = 8

f32 = jnp.float32
bf16 = jnp.bfloat16
highest = lax.Precision.HIGHEST

HBM = pl.BlockSpec(memory_space=pltpu.HBM)
SMEM = pl.BlockSpec(memory_space=pltpu.SMEM)
VMEM = pl.BlockSpec(memory_space=pltpu.VMEM)

LIMIT = pltpu.CompilerParams(vmem_limit_bytes=24 << 20)

NN = (((1,), (0,)), ((), ()))
NT = (((1,), (1,)), ((), ()))
TN = (((0,), (0,)), ((), ()))


def dot(a, b, dims, precision=None):
    return lax.dot_general(a, b, dims, precision=precision, preferred_element_type=f32)


def pieces(x):
    high = x.astype(bf16)
    rest = x - high.astype(f32)
    middle = rest.astype(bf16)
    low = (rest - middle.astype(f32)).astype(bf16)
    return high, middle, low


def in_vmem(x):
    return pltpu.with_memory_space_constraint(x, pltpu.VMEM)


def factor(gram, beside=lambda k: None):
    n = gram.shape[0]
    row = lax.broadcasted_iota(jnp.int32, (n, n), 0)
    col = lax.broadcasted_iota(jnp.int32, (n, n), 1)
    tall = lax.broadcasted_iota(jnp.int32, (PANEL, 2 * n), 0)
    work = jnp.concatenate([gram, (row == col).astype(f32)], axis=1)
    panels = [work[k : k + PANEL] for k in range(0, n, PANEL)]
    for k in range(len(panels)):
        columns = [
            [
                jnp.broadcast_to(panels[t][:, k * PANEL + j : k * PANEL + j + 1], (PANEL, 2 * n))
                for j in range(PANEL)
            ]
            for t in range(k, len(panels))
        ]
        scales = jnp.zeros((PANEL, 2 * n), f32)
        for j in range(PANEL):
            inverse = 1.0 / columns[0][j][j : j + 1]
            scales = jnp.where(tall == j, inverse, scales)
            entries = [columns[0][i][j : j + 1] for i in range(PANEL)]
            pivot_row = panels[k][j : j + 1]
            for t in range(k, len(panels)):
                multiplier = columns[t - k][j] * inverse
                if t == k:
                    if j == PANEL - 1:
                        continue
                    multiplier = jnp.where(tall > j, multiplier, 0.0)
                for i in range(j + 1, PANEL):
                    columns[t - k][i] = columns[t - k][i] - multiplier * entries[i]
                panels[t] = panels[t] - multiplier * pivot_row
            if j == PANEL // 2:
                beside(k)
        panels[k] = panels[k] * jnp.sqrt(scales)
    work = jnp.concatenate(panels, axis=0)
    upper = jnp.where(col >= row, work[:, :n], 0.0)
    return upper, work[:, n:]


def weights_of(x):
    high, middle, low = (piece.astype(f32) for piece in pieces(x))
    lane = lax.broadcasted_iota(jnp.int32, x.shape, 1)
    return jnp.concatenate([jnp.where(lane < RANK, high, middle), low], axis=1).astype(bf16)


def weighted(x, weights):
    terms = dot(x, weights, NN)
    first, last = terms[:, :LANES], terms[:, LANES:]
    return first + pltpu.roll(first, RANK, 1) + last


def folded(x):
    rows = x.shape[0] // 2
    lane = lax.broadcasted_iota(jnp.int32, (rows, LANES), 1)
    return jnp.where(lane < RANK, x[:rows], x[rows:])


def unfolded(x):
    lane = lax.broadcasted_iota(jnp.int32, x.shape, 1)
    turned = pltpu.roll(x, RANK, 1)
    return jnp.concatenate([jnp.where(lane < RANK, x, turned), jnp.where(lane < RANK, turned, x)], axis=0)


class Tile:
    def __init__(self, source, target, sem, strips=8):
        self.whole = pltpu.make_async_copy(source, target, sem)
        rows = source.shape[0] // strips
        self.strips = [
            pltpu.make_async_copy(source.at[pl.ds(k * rows, rows)], target.at[pl.ds(k * rows, rows)], sem)
            for k in range(strips)
        ]

    def start(self):
        for strip in self.strips:
            strip.start()

    def wait(self):
        self.whole.wait()


def mixed_probes_kernel(start, mixing_hbm, probes_ref, out_ref, mixing_ref, tiles_ref, sems):
    part = out_ref.shape[0]
    first = Tile(mixing_hbm, mixing_ref, sems.at[part])
    copies = [Tile(probes_ref.at[start + i], tiles_ref.at[i], sems.at[i]) for i in range(part)]
    for copy in [first] + copies:
        copy.start()
    first.wait()
    mixing = mixing_ref[...]
    weights = weights_of(jnp.concatenate([mixing, mixing], axis=0).T)
    for i, copy in enumerate(copies):
        copy.wait()
        out_ref[i] = folded(weighted(tiles_ref[i], weights))


def mixed_probes(start, part, mixing, probes):
    _, rows, width = probes.shape
    return pl.pallas_call(
        functools.partial(mixed_probes_kernel, start),
        out_shape=pltpu.VMEM((part, rows // 2, LANES), f32),
        in_specs=[HBM, HBM],
        out_specs=VMEM,
        scratch_shapes=[
            pltpu.VMEM(mixing.shape, f32),
            pltpu.VMEM((part, rows, width), bf16),
            pltpu.SemaphoreType.DMA((part + 1,)),
        ],
        cost_estimate=pl.CostEstimate(
            flops=2 * part * rows * width * 3 * RANK,
            bytes_accessed=part * rows * (2 * width + 4 * RANK),
            transcendentals=0,
        ),
        compiler_params=LIMIT,
        name="mixed_probes",
    )(mixing, probes)


def load_kernel(meta_ref, after_ref, tiles_ref, out_ref, sems):
    del meta_ref, after_ref
    part = out_ref.shape[0]
    copies = [Tile(tiles_ref.at[i, 0], out_ref.at[i], sems.at[i]) for i in range(part)]
    for copy in copies:
        copy.start()
    for copy in copies:
        copy.wait()


def load(meta, after, tiles, part):
    _, _, rows, width = tiles.shape
    return pl.pallas_call(
        load_kernel,
        out_shape=pltpu.VMEM((part, rows, width), tiles.dtype),
        in_specs=[SMEM, VMEM, HBM],
        out_specs=VMEM,
        scratch_shapes=[pltpu.SemaphoreType.DMA((part,))],
        cost_estimate=pl.CostEstimate(
            flops=0, bytes_accessed=4 * part * rows * width, transcendentals=0
        ),
        compiler_params=LIMIT,
        name="load",
    )(meta, in_vmem(after), tiles)


def sketch_kernel(
    meta_ref, own_a, own_b, moved_a, moved_b, other_a, other_b, ready_ref, near_ref, keep_ref, send_ref,
    pick_ref, tiles_ref, sems
):
    count = near_ref.shape[0]
    ready = ready_ref.shape[0]
    copies = [Tile(near_ref.at[ready + i, 0], tiles_ref.at[i], sems.at[i]) for i in range(count - ready)]
    for copy in copies:
        copy.start()
    part = own_a.shape[0]
    core = meta_ref[2 * count]
    sources = (
        (own_a, 2), (own_b, 3), (moved_a, 4 * core), (moved_b, 4 * core + 1),
        (other_a, 4 - 4 * core), (other_b, 5 - 4 * core),
    )

    def pick(i):
        column = jnp.clip(meta_ref[i], 0, 6 * part - 1)
        for source, group in sources:

            @pl.when(column // part == group)
            def _():
                pick_ref[i] = source[column % part]

    for i in range(count):
        pick(i)
    for i in range(count):
        if i >= ready:
            copies[i - ready].wait()
        tile = ready_ref[i] if i < ready else tiles_ref[i - ready]
        mixed = folded(weighted(tile, weights_of(unfolded(pick_ref[i]))))
        mixed = jnp.where(meta_ref[count + i] > 0, mixed, 0.0)
        rows = mixed.shape[0] // 2
        keep_ref[i] = jnp.where(core == 0, mixed[:rows], mixed[rows:])
        send_ref[i] = jnp.where(core == 0, mixed[rows:], mixed[:rows])


def compress(meta, parts, ready, near_tiles):
    count, _, rows, width = near_tiles.shape
    shape = pltpu.VMEM((count, rows // 4, LANES), f32)
    return pl.pallas_call(
        sketch_kernel,
        out_shape=(shape, shape),
        in_specs=[SMEM] + [VMEM] * 7 + [HBM],
        out_specs=(VMEM, VMEM),
        scratch_shapes=[
            pltpu.VMEM((count, rows // 2, LANES), f32),
            pltpu.VMEM((count - ready.shape[0], rows, width), bf16),
            pltpu.SemaphoreType.DMA((count - ready.shape[0],)),
        ],
        cost_estimate=pl.CostEstimate(
            flops=2 * count * rows * width * 3 * RANK,
            bytes_accessed=count * rows * (2 * width + 16 * RANK),
            transcendentals=0,
        ),
        compiler_params=LIMIT,
        name="compress",
    )(meta, *[in_vmem(x) for x in (*parts, ready)], near_tiles)


def gram_kernel(terms_ref, mixed_ref, gram_ref):
    total = terms_ref[0]
    for k in range(1, terms_ref.shape[0]):
        total = total + terms_ref[k]
    mixed = total.T
    mixed_ref[...] = mixed
    first, second = mixed[:RANK], mixed[RANK:]
    gram_ref[...] = dot(first, first, NT, highest) + dot(second, second, NT, highest)


def gram_of(terms):
    return pl.pallas_call(
        gram_kernel,
        out_shape=(
            pltpu.VMEM((terms.shape[2], terms.shape[1]), f32),
            pltpu.VMEM((RANK, RANK), f32),
        ),
        in_specs=[VMEM],
        out_specs=(VMEM, VMEM),
        compiler_params=LIMIT,
        name="gram",
    )(in_vmem(terms))


def basis_kernel(core_ref, mixed_ref, gram_ref, other_ref, out_ref):
    upper, inverse = factor(gram_ref[...] + other_ref[...])
    basis = [dot(inverse, mixed_ref[k : k + RANK], NN, highest) for k in (0, RANK)]
    half = RANK // 2
    rows = jnp.where(core_ref[0] == 0, upper[:half], upper[half:])
    high, middle, low = (piece.astype(f32) for piece in pieces(rows))
    left = jnp.concatenate([high, middle], axis=0)
    right = jnp.concatenate([low, jnp.zeros_like(low)], axis=0)
    block = jnp.concatenate(basis + [left, right], axis=1).astype(bf16)
    for k in range(out_ref.shape[0]):
        out_ref[k] = block


def basis_of(core, mixed, gram, other, copies):
    return pl.pallas_call(
        basis_kernel,
        out_shape=pltpu.VMEM((copies, RANK, 2 * mixed.shape[1] + LANES), bf16),
        in_specs=[SMEM, VMEM, VMEM, VMEM],
        out_specs=VMEM,
        compiler_params=LIMIT,
        name="basis",
    )(core, in_vmem(mixed), in_vmem(gram), in_vmem(other))


def upper_half(block, width):
    half = RANK // 2
    left = block[:, width : width + RANK]
    return left[:half] + left[half:] + block[:half, width + RANK :]


def spread_kernel(far_ref, own_ref, out_ref, work_ref):
    count = own_ref.shape[0]
    groups = out_ref.shape[0] // count
    blocks = RANK // groups
    width = own_ref.shape[2] - LANES
    wide = width // LANES
    tiles = work_ref.shape[0]
    total = jnp.zeros((RANK, RANK), f32)
    for r in range(count):
        block = own_ref[r].astype(f32)
        for q in range(blocks):
            for t in range(wide):
                work_ref[q * wide + t, pl.ds(r, groups, stride=count), :] = block[
                    q * groups : (q + 1) * groups, t * LANES : (t + 1) * LANES
                ]
        upper = upper_half(block, width)
        total = total + dot(upper, upper, TN, highest)
        work_ref[tiles - 2, pl.ds(r, groups, stride=count), :] = jnp.full(
            (groups, LANES), far_ref[r].astype(f32), f32
        )
    work_ref[tiles - 1] = jnp.zeros((groups * count, LANES), f32)
    for p in range(2):
        low_row = 2 * p * groups
        packed = jnp.concatenate(
            [total[low_row : low_row + groups], total[low_row + groups : low_row + 2 * groups]], axis=1
        )
        for k, piece in enumerate(pieces(packed)):
            work_ref[tiles - 1, pl.ds(2 * k + p, groups, stride=count), :] = piece.astype(f32)
    for t in range(tiles):
        out_ref[:, t * LANES : (t + 1) * LANES] = work_ref[t].astype(bf16)


def spread(far, own, groups):
    count, _, width = own.shape
    total = RANK // groups * (width - LANES) + 2 * LANES
    return pl.pallas_call(
        spread_kernel,
        out_shape=pltpu.VMEM((groups * count, total), bf16),
        in_specs=[SMEM, VMEM],
        out_specs=VMEM,
        scratch_shapes=[pltpu.VMEM((total // LANES, groups * count, LANES), f32)],
        compiler_params=LIMIT,
        name="spread",
    )(far, in_vmem(own))


def choose_kernel(count, core_ref, own_ref, other_ref, out_ref):
    clusters, total = own_ref.shape
    body = total - 2 * LANES
    first = core_ref[0] == 0
    wanted = own_ref[:, body : body + LANES].astype(f32)
    column = lax.broadcasted_iota(jnp.int32, (clusters, clusters), 1).astype(f32)
    select = (wanted == column).astype(bf16)
    own = dot(select, own_ref[:, :body], NN)
    other = dot(select, other_ref[:, :body], NN)
    for t in range(body // LANES):
        mine, others = own[:, t * LANES : (t + 1) * LANES], other[:, t * LANES : (t + 1) * LANES]
        out_ref[:, 2 * t * LANES : (2 * t + 1) * LANES] = jnp.where(first, mine, others).astype(bf16)
        out_ref[:, (2 * t + 1) * LANES : (2 * t + 2) * LANES] = jnp.where(first, others, mine).astype(bf16)
    row = lax.broadcasted_iota(jnp.int32, (count, clusters), 0)
    column = lax.broadcasted_iota(jnp.int32, (count, clusters), 1) % count
    gather = (((column == row) | (column == row + 2) | (column == row + 4)) & (row < 2)).astype(bf16)
    sums = (dot(gather, own_ref[:, body + LANES :], NN) + dot(gather, other_ref[:, body + LANES :], NN))[:2]
    block = jnp.concatenate([piece.astype(f32) for piece in pieces(sums)] + [jnp.zeros((count - 6, LANES), f32)], axis=0)
    out_ref[:, 2 * body :] = jnp.concatenate([block] * (clusters // count), axis=0).astype(bf16)


def choose(core, own, other, count):
    rows, total = own.shape
    return pl.pallas_call(
        functools.partial(choose_kernel, count),
        out_shape=pltpu.VMEM((rows, 2 * (total - 2 * LANES) + LANES), bf16),
        in_specs=[SMEM, VMEM, VMEM],
        out_specs=VMEM,
        compiler_params=LIMIT,
        name="choose",
    )(core, in_vmem(own), in_vmem(other))


def project_kernel(core_ref, own_ref, other_ref, far_ref, out_ref, upper_ref):
    count = own_ref.shape[0]
    first = core_ref[0] == 0
    half = own_ref.shape[2] - LANES
    for i in range(count):
        mine, others = own_ref[i].astype(f32), other_ref[i].astype(f32)
        sides = (jnp.where(first, mine, others), jnp.where(first, others, mine))
        basis = [side[:, t : t + LANES] for t in range(0, half, LANES) for side in sides]
        image = dot(jnp.concatenate(basis, axis=1).astype(bf16), far_ref[i, 0], NN)
        out_ref[i] = jnp.concatenate(pieces(image), axis=0)
        upper_ref[i] = jnp.concatenate([upper_half(side, half) for side in sides], axis=0)


def project(core, own, other, far_tiles):
    count, _, rows, width = far_tiles.shape
    return pl.pallas_call(
        project_kernel,
        out_shape=(
            pltpu.VMEM((count, 3 * RANK, width), bf16),
            pltpu.VMEM((count, RANK, RANK), f32),
        ),
        in_specs=[SMEM] + [VMEM] * 3,
        out_specs=(VMEM, VMEM),
        cost_estimate=pl.CostEstimate(
            flops=2 * count * rows * width * RANK,
            bytes_accessed=count * rows * width * 4,
            transcendentals=0,
        ),
        compiler_params=LIMIT,
        name="project",
    )(core, *[in_vmem(x) for x in (own, other, far_tiles)])


def couple_kernel(scale, image_ref, upper_ref, received_ref, coupling_ref, root_ref, work_ref):
    count = image_ref.shape[0]
    rows, total = received_ref.shape
    groups = rows // count
    blocks = RANK // groups
    wide = (total - LANES) // blocks // LANES
    tiles = work_ref.shape[0]
    for t in range(tiles):
        work_ref[t] = received_ref[:, t * LANES : (t + 1) * LANES].astype(f32)
    parts = []
    for p in range(2):
        packed = sum(work_ref[tiles - 1, pl.ds(2 * k + p, groups, stride=count), :] for k in range(3))
        parts += [packed[:, :RANK], packed[:, RANK:]]

    def coupling(i):
        far = [
            jnp.concatenate(
                [work_ref[q * wide + t, pl.ds(i, groups, stride=count), :] for t in range(wide)], axis=1
            )
            for q in range(blocks)
        ]
        terms = dot(image_ref[i], jnp.concatenate(far, axis=0).astype(bf16), NT)
        coupling_ref[i, 0] = terms[:RANK] + terms[RANK : 2 * RANK] + terms[2 * RANK :]

    _, inverse = factor(jnp.concatenate(parts, axis=0), coupling)
    for i in range(count):
        root_ref[i] = dot(upper_ref[i], inverse, NT, highest) * scale


def couple(image, upper, received, scale):
    count = image.shape[0]
    return pl.pallas_call(
        functools.partial(couple_kernel, scale),
        out_shape=(
            jax.ShapeDtypeStruct((count, 1, RANK, RANK), f32),
            jax.ShapeDtypeStruct((count, RANK, RANK), f32),
        ),
        in_specs=[VMEM] * 3,
        out_specs=(VMEM, VMEM),
        scratch_shapes=[pltpu.VMEM((received.shape[1] // LANES, received.shape[0], LANES), f32)],
        compiler_params=LIMIT,
        name="couple",
    )(*[in_vmem(x) for x in (image, upper, received)])


def shards(near_tiles, near_cols, near_count, probes, mixing, far_tiles, far_cols):
    count = probes.shape[0]
    subtrees = lax.axis_size("leaf")
    members = lax.axis_size("blk")
    leaf_pos = lax.axis_index("leaf")
    blk_pos = lax.axis_index("blk")
    core = blk_pos % 2
    pair = [(i, i ^ 1) for i in range(members)]
    lanes = [list(range(c, members, 2)) for c in range(2)]
    shift = [
        (g * members + b, (g + step) * members + b)
        for g in range(subtrees)
        for b in range(members)
        for step in [1 - 2 * (b % 2)]
        if 0 <= g + step < subtrees
    ]

    core = core.reshape(1).astype(jnp.int32)
    live = (blk_pos < near_count).astype(jnp.int32)
    near_meta = jnp.concatenate([near_cols[:, 0] - (leaf_pos * count - REACH), live, core])

    mixing, probes = (pltpu.with_memory_space_constraint(x, pltpu.HBM) for x in (mixing.T, probes))
    part = count // 2
    own = [mixed_probes(start, part, mixing, probes) for start in (0, part)]
    moved = [lax.ppermute(x, ("leaf", "blk"), shift) for x in own]
    other = [lax.ppermute(x, "blk", pair) for x in moved]
    near_tiles = pltpu.with_memory_space_constraint(near_tiles, pltpu.HBM)
    ready = load(near_meta, own[1], near_tiles, part)
    keep, send = compress(near_meta, own + moved + other, ready, near_tiles)
    halves = keep + lax.ppermute(send, "blk", pair)
    terms = lax.all_to_all(halves, "blk", 0, 0, tiled=True, axis_index_groups=lanes)
    mixed, gram = gram_of(terms)
    own = basis_of(core, mixed, gram, lax.ppermute(gram, "blk", pair), count)
    own = lax.all_to_all(own, "blk", 0, 0, tiled=True, axis_index_groups=lanes)
    other = lax.ppermute(own, "blk", pair)
    payload = spread(far_cols[:, 0], own, subtrees)
    slices = lax.all_to_all(payload.reshape(subtrees, count, -1), "leaf", 0, 0, tiled=True)
    slices = slices.reshape(payload.shape)
    image, upper = project(core, own, other, far_tiles)
    chosen = choose(core, slices, lax.ppermute(slices, "blk", pair), count)
    received = lax.all_to_all(chosen.reshape(subtrees, count, -1), "leaf", 0, 0, tiled=True)
    scale = math.sqrt(subtrees * count * RANK)
    return couple(image, upper, received.reshape(chosen.shape), scale)


def solution(mesh):
    in_specs = (
        P("leaf", "blk", None, None),
        P("leaf", "blk"),
        P("leaf"),
        P("leaf", None, None),
        P(),
        P("leaf", "blk", None, None),
        P("leaf", "blk"),
    )
    out_specs = (P("leaf", "blk", None, None), P("leaf", None, None))
    return jax.shard_map(shards, mesh=mesh, in_specs=in_specs, out_specs=out_specs, check_vma=False)
```

```python
import functools
import math

import jax
import jax.numpy as jnp
from jax import lax
from jax.experimental import pallas as pl
from jax.experimental.pallas import tpu as pltpu
from jax.sharding import PartitionSpec as P

RANK = 64
REACH = 8
LANES = 128
PANEL = 8

f32 = jnp.float32
bf16 = jnp.bfloat16
highest = lax.Precision.HIGHEST

HBM = pl.BlockSpec(memory_space=pltpu.HBM)
SMEM = pl.BlockSpec(memory_space=pltpu.SMEM)
VMEM = pl.BlockSpec(memory_space=pltpu.VMEM)

LIMIT = pltpu.CompilerParams(vmem_limit_bytes=24 << 20)

NN = (((1,), (0,)), ((), ()))
NT = (((1,), (1,)), ((), ()))
TN = (((0,), (0,)), ((), ()))


def dot(a, b, dims, precision=None):
    return lax.dot_general(a, b, dims, precision=precision, preferred_element_type=f32)


def pieces(x):
    high = x.astype(bf16)
    rest = x - high.astype(f32)
    middle = rest.astype(bf16)
    low = (rest - middle.astype(f32)).astype(bf16)
    return high, middle, low


def in_vmem(x):
    return pltpu.with_memory_space_constraint(x, pltpu.VMEM)


def factor(gram):
    n = gram.shape[0]
    row = lax.broadcasted_iota(jnp.int32, (n, n), 0)
    col = lax.broadcasted_iota(jnp.int32, (n, n), 1)
    tall = lax.broadcasted_iota(jnp.int32, (PANEL, 2 * n), 0)
    work = jnp.concatenate([gram, (row == col).astype(f32)], axis=1)
    panels = [work[k : k + PANEL] for k in range(0, n, PANEL)]
    for k in range(len(panels)):
        columns = [
            [
                jnp.broadcast_to(panels[t][:, k * PANEL + j : k * PANEL + j + 1], (PANEL, 2 * n))
                for j in range(PANEL)
            ]
            for t in range(k, len(panels))
        ]
        scales = jnp.zeros((PANEL, 2 * n), f32)
        for j in range(PANEL):
            inverse = 1.0 / columns[0][j][j : j + 1]
            scales = jnp.where(tall == j, inverse, scales)
            entries = [columns[0][i][j : j + 1] for i in range(PANEL)]
            pivot_row = panels[k][j : j + 1]
            for t in range(k, len(panels)):
                multiplier = columns[t - k][j] * inverse
                if t == k:
                    if j == PANEL - 1:
                        continue
                    multiplier = jnp.where(tall > j, multiplier, 0.0)
                for i in range(j + 1, PANEL):
                    columns[t - k][i] = columns[t - k][i] - multiplier * entries[i]
                panels[t] = panels[t] - multiplier * pivot_row
        panels[k] = panels[k] * jnp.sqrt(scales)
    work = jnp.concatenate(panels, axis=0)
    upper = jnp.where(col >= row, work[:, :n], 0.0)
    return upper, work[:, n:]


def weights_of(x):
    high, middle, low = (piece.astype(f32) for piece in pieces(x))
    lane = lax.broadcasted_iota(jnp.int32, x.shape, 1)
    return jnp.concatenate([jnp.where(lane < RANK, high, middle), low], axis=1).astype(bf16)


def weighted(x, weights):
    terms = dot(x, weights, NN)
    first, last = terms[:, :LANES], terms[:, LANES:]
    return first + pltpu.roll(first, RANK, 1) + last


def folded(x):
    rows = x.shape[0] // 2
    lane = lax.broadcasted_iota(jnp.int32, (rows, LANES), 1)
    return jnp.where(lane < RANK, x[:rows], x[rows:])


def unfolded(x):
    lane = lax.broadcasted_iota(jnp.int32, x.shape, 1)
    turned = pltpu.roll(x, RANK, 1)
    return jnp.concatenate([jnp.where(lane < RANK, x, turned), jnp.where(lane < RANK, turned, x)], axis=0)


def first_probes_kernel(mixing_hbm, probes_ref, out_ref, rest_ref, weights_ref, mixing_ref, tiles_ref, sems):
    part = out_ref.shape[0]
    first = pltpu.make_async_copy(mixing_hbm, mixing_ref, sems.at[2 * part])
    copies = [pltpu.make_async_copy(probes_ref.at[i], tiles_ref.at[i], sems.at[i]) for i in range(part)]
    later = [
        pltpu.make_async_copy(probes_ref.at[part + i], rest_ref.at[i], sems.at[part + i])
        for i in range(rest_ref.shape[0])
    ]
    for copy in [first] + copies + later:
        copy.start()
    first.wait()
    mixing = mixing_ref[...]
    weights = weights_of(jnp.concatenate([mixing, mixing], axis=0).T)
    weights_ref[...] = weights
    for i, copy in enumerate(copies):
        copy.wait()
        out_ref[i] = folded(weighted(tiles_ref[i], weights))
    for copy in later:
        copy.wait()


def rest_probes_kernel(rest_ref, weights_ref, out_ref):
    for i in range(out_ref.shape[0]):
        out_ref[i] = folded(weighted(rest_ref[i], weights_ref[...]))


def mixed_probes(mixing, probes):
    count, rows, width = probes.shape
    part = count // 2
    half = pltpu.VMEM((part, rows // 2, LANES), f32)
    cost = pl.CostEstimate(
        flops=2 * part * rows * width * 3 * RANK,
        bytes_accessed=part * rows * (2 * width + 4 * RANK),
        transcendentals=0,
    )
    first, rest, weights = pl.pallas_call(
        first_probes_kernel,
        out_shape=(
            half,
            pltpu.VMEM((count - part, rows, width), bf16),
            pltpu.VMEM((width, 2 * LANES), bf16),
        ),
        in_specs=[HBM, HBM],
        out_specs=(VMEM, VMEM, VMEM),
        scratch_shapes=[
            pltpu.VMEM(mixing.shape, f32),
            pltpu.VMEM((part, rows, width), bf16),
            pltpu.SemaphoreType.DMA((2 * part + 1,)),
        ],
        cost_estimate=cost,
        compiler_params=LIMIT,
        name="first_probes",
    )(mixing, probes)
    second = pl.pallas_call(
        rest_probes_kernel,
        out_shape=half,
        in_specs=[VMEM, VMEM],
        out_specs=VMEM,
        cost_estimate=cost,
        compiler_params=LIMIT,
        name="rest_probes",
    )(in_vmem(rest), in_vmem(weights))
    return [first, second]


def load_kernel(*refs):
    count = len(refs) // 2
    sems = refs[-1]
    copies = [
        pltpu.make_async_copy(refs[k], refs[count + k], sems.at[k]) for k in range(count)
    ]
    for copy in copies:
        copy.start()
    for copy in copies:
        copy.wait()


def load(meta, after, *arrays):
    def kernel(meta_ref, after_ref, *refs):
        load_kernel(*refs)

    arrays = [pltpu.with_memory_space_constraint(x, pltpu.HBM) for x in arrays]
    return pl.pallas_call(
        kernel,
        out_shape=tuple(pltpu.VMEM(x.shape, x.dtype) for x in arrays),
        in_specs=[SMEM, VMEM] + [HBM] * len(arrays),
        out_specs=(VMEM,) * len(arrays),
        scratch_shapes=[pltpu.SemaphoreType.DMA((len(arrays),))],
        cost_estimate=pl.CostEstimate(
            flops=0, bytes_accessed=2 * sum(x.size * x.dtype.itemsize for x in arrays), transcendentals=0
        ),
        compiler_params=LIMIT,
        name="load",
    )(meta, in_vmem(after), *arrays)


def sketch_kernel(
    meta_ref, own_a, own_b, moved_a, moved_b, other_a, other_b, near_ref, keep_ref, send_ref, pick_ref
):
    count = near_ref.shape[0]
    part = own_a.shape[0]
    core = meta_ref[2 * count]
    sources = (
        (own_a, 2), (own_b, 3), (moved_a, 4 * core), (moved_b, 4 * core + 1),
        (other_a, 4 - 4 * core), (other_b, 5 - 4 * core),
    )

    def pick(i):
        column = jnp.clip(meta_ref[i], 0, 6 * part - 1)
        for source, group in sources:

            @pl.when(column // part == group)
            def _():
                pick_ref[i] = source[column % part]

    for i in range(count):
        pick(i)
    for i in range(count):
        mixed = folded(weighted(near_ref[i, 0], weights_of(unfolded(pick_ref[i]))))
        mixed = jnp.where(meta_ref[count + i] > 0, mixed, 0.0)
        rows = mixed.shape[0] // 2
        keep_ref[i] = jnp.where(core == 0, mixed[:rows], mixed[rows:])
        send_ref[i] = jnp.where(core == 0, mixed[rows:], mixed[:rows])


def compress(meta, parts, near_tiles):
    count, _, rows, width = near_tiles.shape
    shape = pltpu.VMEM((count, rows // 4, LANES), f32)
    return pl.pallas_call(
        sketch_kernel,
        out_shape=(shape, shape),
        in_specs=[SMEM] + [VMEM] * 7,
        out_specs=(VMEM, VMEM),
        scratch_shapes=[pltpu.VMEM((count, rows // 2, LANES), f32)],
        cost_estimate=pl.CostEstimate(
            flops=2 * count * rows * width * 3 * RANK,
            bytes_accessed=count * rows * (2 * width + 16 * RANK),
            transcendentals=0,
        ),
        compiler_params=LIMIT,
        name="compress",
    )(meta, *[in_vmem(part) for part in parts], in_vmem(near_tiles))


def gram_kernel(terms_ref, mixed_ref, gram_ref):
    total = terms_ref[0]
    for k in range(1, terms_ref.shape[0]):
        total = total + terms_ref[k]
    mixed = total.T
    mixed_ref[...] = mixed
    first, second = mixed[:RANK], mixed[RANK:]
    gram_ref[...] = dot(first, first, NT, highest) + dot(second, second, NT, highest)


def gram_of(terms):
    return pl.pallas_call(
        gram_kernel,
        out_shape=(
            pltpu.VMEM((terms.shape[2], terms.shape[1]), f32),
            pltpu.VMEM((RANK, RANK), f32),
        ),
        in_specs=[VMEM],
        out_specs=(VMEM, VMEM),
        compiler_params=LIMIT,
        name="gram",
    )(in_vmem(terms))


def basis_kernel(core_ref, mixed_ref, gram_ref, other_ref, out_ref):
    upper, inverse = factor(gram_ref[...] + other_ref[...])
    basis = [dot(inverse, mixed_ref[k : k + RANK], NN, highest) for k in (0, RANK)]
    half = RANK // 2
    rows = jnp.where(core_ref[0] == 0, upper[:half], upper[half:])
    high, middle, low = (piece.astype(f32) for piece in pieces(rows))
    left = jnp.concatenate([high, middle], axis=0)
    right = jnp.concatenate([low, jnp.zeros_like(low)], axis=0)
    block = jnp.concatenate(basis + [left, right], axis=1).astype(bf16)
    for k in range(out_ref.shape[0]):
        out_ref[k] = block


def basis_of(core, mixed, gram, other, copies):
    return pl.pallas_call(
        basis_kernel,
        out_shape=pltpu.VMEM((copies, RANK, 2 * mixed.shape[1] + LANES), bf16),
        in_specs=[SMEM, VMEM, VMEM, VMEM],
        out_specs=VMEM,
        compiler_params=LIMIT,
        name="basis",
    )(core, in_vmem(mixed), in_vmem(gram), in_vmem(other))


def upper_half(block, width):
    half = RANK // 2
    left = block[:, width : width + RANK]
    return left[:half] + left[half:] + block[:half, width + RANK :]


def spread_kernel(far_ref, own_ref, out_ref, work_ref):
    count = own_ref.shape[0]
    groups = out_ref.shape[0] // count
    blocks = RANK // groups
    width = own_ref.shape[2] - LANES
    wide = width // LANES
    tiles = work_ref.shape[0]
    total = jnp.zeros((RANK, RANK), f32)
    for r in range(count):
        block = own_ref[r].astype(f32)
        for q in range(blocks):
            for t in range(wide):
                work_ref[q * wide + t, pl.ds(r, groups, stride=count), :] = block[
                    q * groups : (q + 1) * groups, t * LANES : (t + 1) * LANES
                ]
        upper = upper_half(block, width)
        total = total + dot(upper, upper, TN, highest)
        work_ref[tiles - 2, pl.ds(r, groups, stride=count), :] = jnp.full(
            (groups, LANES), far_ref[r].astype(f32), f32
        )
    work_ref[tiles - 1] = jnp.zeros((groups * count, LANES), f32)
    for p in range(2):
        low_row = 2 * p * groups
        packed = jnp.concatenate(
            [total[low_row : low_row + groups], total[low_row + groups : low_row + 2 * groups]], axis=1
        )
        for k, piece in enumerate(pieces(packed)):
            work_ref[tiles - 1, pl.ds(2 * k + p, groups, stride=count), :] = piece.astype(f32)
    for t in range(tiles):
        out_ref[:, t * LANES : (t + 1) * LANES] = work_ref[t].astype(bf16)


def spread(far, own, groups):
    count, _, width = own.shape
    total = RANK // groups * (width - LANES) + 2 * LANES
    return pl.pallas_call(
        spread_kernel,
        out_shape=pltpu.VMEM((groups * count, total), bf16),
        in_specs=[SMEM, VMEM],
        out_specs=VMEM,
        scratch_shapes=[pltpu.VMEM((total // LANES, groups * count, LANES), f32)],
        compiler_params=LIMIT,
        name="spread",
    )(far, in_vmem(own))


def choose_kernel(count, core_ref, own_ref, other_ref, out_ref):
    clusters, total = own_ref.shape
    body = total - 2 * LANES
    first = core_ref[0] == 0
    wanted = own_ref[:, body : body + LANES].astype(f32)
    column = lax.broadcasted_iota(jnp.int32, (clusters, clusters), 1).astype(f32)
    select = (wanted == column).astype(bf16)
    own = dot(select, own_ref[:, :body], NN)
    other = dot(select, other_ref[:, :body], NN)
    for t in range(body // LANES):
        mine, others = own[:, t * LANES : (t + 1) * LANES], other[:, t * LANES : (t + 1) * LANES]
        out_ref[:, 2 * t * LANES : (2 * t + 1) * LANES] = jnp.where(first, mine, others).astype(bf16)
        out_ref[:, (2 * t + 1) * LANES : (2 * t + 2) * LANES] = jnp.where(first, others, mine).astype(bf16)
    row = lax.broadcasted_iota(jnp.int32, (count, clusters), 0)
    column = lax.broadcasted_iota(jnp.int32, (count, clusters), 1) % count
    gather = (((column == row) | (column == row + 2) | (column == row + 4)) & (row < 2)).astype(bf16)
    sums = (dot(gather, own_ref[:, body + LANES :], NN) + dot(gather, other_ref[:, body + LANES :], NN))[:2]
    block = jnp.concatenate([piece.astype(f32) for piece in pieces(sums)] + [jnp.zeros((count - 6, LANES), f32)], axis=0)
    out_ref[:, 2 * body :] = jnp.concatenate([block] * (clusters // count), axis=0).astype(bf16)


def choose(core, own, other, count):
    rows, total = own.shape
    return pl.pallas_call(
        functools.partial(choose_kernel, count),
        out_shape=pltpu.VMEM((rows, 2 * (total - 2 * LANES) + LANES), bf16),
        in_specs=[SMEM, VMEM, VMEM],
        out_specs=VMEM,
        compiler_params=LIMIT,
        name="choose",
    )(core, in_vmem(own), in_vmem(other))


def project_kernel(core_ref, own_ref, other_ref, far_ref, out_ref, upper_ref):
    count = own_ref.shape[0]
    first = core_ref[0] == 0
    half = own_ref.shape[2] - LANES
    for i in range(count):
        mine, others = own_ref[i].astype(f32), other_ref[i].astype(f32)
        sides = (jnp.where(first, mine, others), jnp.where(first, others, mine))
        basis = [side[:, t : t + LANES] for t in range(0, half, LANES) for side in sides]
        image = dot(jnp.concatenate(basis, axis=1).astype(bf16), far_ref[i, 0], NN)
        out_ref[i] = jnp.concatenate(pieces(image), axis=0)
        upper_ref[i] = jnp.concatenate([upper_half(side, half) for side in sides], axis=0)


def project(core, own, other, far_tiles):
    count, _, rows, width = far_tiles.shape
    return pl.pallas_call(
        project_kernel,
        out_shape=(
            pltpu.VMEM((count, 3 * RANK, width), bf16),
            pltpu.VMEM((count, RANK, RANK), f32),
        ),
        in_specs=[SMEM] + [VMEM] * 3,
        out_specs=(VMEM, VMEM),
        cost_estimate=pl.CostEstimate(
            flops=2 * count * rows * width * RANK,
            bytes_accessed=count * rows * width * 4,
            transcendentals=0,
        ),
        compiler_params=LIMIT,
        name="project",
    )(core, *[in_vmem(x) for x in (own, other, far_tiles)])


def couple_kernel(scale, image_ref, upper_ref, received_ref, coupling_ref, root_ref, work_ref):
    count = image_ref.shape[0]
    rows, total = received_ref.shape
    groups = rows // count
    blocks = RANK // groups
    wide = (total - LANES) // blocks // LANES
    tiles = work_ref.shape[0]
    for t in range(tiles):
        work_ref[t] = received_ref[:, t * LANES : (t + 1) * LANES].astype(f32)
    parts = []
    for p in range(2):
        packed = sum(work_ref[tiles - 1, pl.ds(2 * k + p, groups, stride=count), :] for k in range(3))
        parts += [packed[:, :RANK], packed[:, RANK:]]
    _, inverse = factor(jnp.concatenate(parts, axis=0))
    for i in range(count):
        far = [
            jnp.concatenate(
                [work_ref[q * wide + t, pl.ds(i, groups, stride=count), :] for t in range(wide)], axis=1
            )
            for q in range(blocks)
        ]
        terms = dot(image_ref[i], jnp.concatenate(far, axis=0).astype(bf16), NT)
        coupling_ref[i, 0] = terms[:RANK] + terms[RANK : 2 * RANK] + terms[2 * RANK :]
    for i in range(count):
        root_ref[i] = dot(upper_ref[i], inverse, NT, highest) * scale


def couple(image, upper, received, scale):
    count = image.shape[0]
    return pl.pallas_call(
        functools.partial(couple_kernel, scale),
        out_shape=(
            jax.ShapeDtypeStruct((count, 1, RANK, RANK), f32),
            jax.ShapeDtypeStruct((count, RANK, RANK), f32),
        ),
        in_specs=[VMEM] * 3,
        out_specs=(VMEM, VMEM),
        scratch_shapes=[pltpu.VMEM((received.shape[1] // LANES, received.shape[0], LANES), f32)],
        compiler_params=LIMIT,
        name="couple",
    )(*[in_vmem(x) for x in (image, upper, received)])


def shards(near_tiles, near_cols, near_count, probes, mixing, far_tiles, far_cols):
    count = probes.shape[0]
    subtrees = lax.axis_size("leaf")
    members = lax.axis_size("blk")
    leaf_pos = lax.axis_index("leaf")
    blk_pos = lax.axis_index("blk")
    core = blk_pos % 2
    pair = [(i, i ^ 1) for i in range(members)]
    lanes = [list(range(c, members, 2)) for c in range(2)]
    shift = [
        (g * members + b, (g + step) * members + b)
        for g in range(subtrees)
        for b in range(members)
        for step in [1 - 2 * (b % 2)]
        if 0 <= g + step < subtrees
    ]

    core = core.reshape(1).astype(jnp.int32)
    live = (blk_pos < near_count).astype(jnp.int32)
    near_meta = jnp.concatenate([near_cols[:, 0] - (leaf_pos * count - REACH), live, core])

    mixing, probes = (pltpu.with_memory_space_constraint(x, pltpu.HBM) for x in (mixing.T, probes))
    own = mixed_probes(mixing, probes)
    moved = [lax.ppermute(x, ("leaf", "blk"), shift) for x in own]
    other = [lax.ppermute(moved[0], "blk", pair)]
    (near_tiles,) = load(near_meta, other[0], near_tiles)
    moved[1], near_tiles = lax.optimization_barrier((moved[1], near_tiles))
    other.append(lax.ppermute(moved[1], "blk", pair))
    keep, send = compress(near_meta, own + moved + other, near_tiles)
    halves = keep + lax.ppermute(send, "blk", pair)
    terms = lax.all_to_all(halves, "blk", 0, 0, tiled=True, axis_index_groups=lanes)
    mixed, gram = gram_of(terms)
    own = basis_of(core, mixed, gram, lax.ppermute(gram, "blk", pair), count)
    own = lax.all_to_all(own, "blk", 0, 0, tiled=True, axis_index_groups=lanes)
    other = lax.ppermute(own, "blk", pair)
    payload = spread(far_cols[:, 0], own, subtrees)
    slices = lax.all_to_all(payload.reshape(subtrees, count, -1), "leaf", 0, 0, tiled=True)
    slices = slices.reshape(payload.shape)
    image, upper = project(core, own, other, far_tiles)
    chosen = choose(core, slices, lax.ppermute(slices, "blk", pair), count)
    received = lax.all_to_all(chosen.reshape(subtrees, count, -1), "leaf", 0, 0, tiled=True)
    scale = math.sqrt(subtrees * count * RANK)
    return couple(image, upper, received.reshape(chosen.shape), scale)


def solution(mesh):
    in_specs = (
        P("leaf", "blk", None, None),
        P("leaf", "blk"),
        P("leaf"),
        P("leaf", None, None),
        P(),
        P("leaf", "blk", None, None),
        P("leaf", "blk"),
    )
    out_specs = (P("leaf", "blk", None, None), P("leaf", None, None))
    return jax.shard_map(shards, mesh=mesh, in_specs=in_specs, out_specs=out_specs, check_vma=False)
```

```python
import functools
import math

import jax
import jax.numpy as jnp
from jax import lax
from jax.experimental import pallas as pl
from jax.experimental.pallas import tpu as pltpu
from jax.sharding import PartitionSpec as P

RANK = 64
REACH = 8
LANES = 128
PANEL = 8

f32 = jnp.float32
bf16 = jnp.bfloat16
highest = lax.Precision.HIGHEST

HBM = pl.BlockSpec(memory_space=pltpu.HBM)
SMEM = pl.BlockSpec(memory_space=pltpu.SMEM)
VMEM = pl.BlockSpec(memory_space=pltpu.VMEM)

LIMIT = pltpu.CompilerParams(vmem_limit_bytes=24 << 20)

NN = (((1,), (0,)), ((), ()))
NT = (((1,), (1,)), ((), ()))
TN = (((0,), (0,)), ((), ()))


def dot(a, b, dims, precision=None):
    return lax.dot_general(a, b, dims, precision=precision, preferred_element_type=f32)


def pieces(x):
    high = x.astype(bf16)
    rest = x - high.astype(f32)
    middle = rest.astype(bf16)
    low = (rest - middle.astype(f32)).astype(bf16)
    return high, middle, low


def in_vmem(x):
    return pltpu.with_memory_space_constraint(x, pltpu.VMEM)


def factor(gram):
    n = gram.shape[0]
    row = lax.broadcasted_iota(jnp.int32, (n, n), 0)
    col = lax.broadcasted_iota(jnp.int32, (n, n), 1)
    tall = lax.broadcasted_iota(jnp.int32, (PANEL, 2 * n), 0)
    work = jnp.concatenate([gram, (row == col).astype(f32)], axis=1)
    panels = [work[k : k + PANEL] for k in range(0, n, PANEL)]
    for k in range(len(panels)):
        columns = [
            [
                jnp.broadcast_to(panels[t][:, k * PANEL + j : k * PANEL + j + 1], (PANEL, 2 * n))
                for j in range(PANEL)
            ]
            for t in range(k, len(panels))
        ]
        scales = jnp.zeros((PANEL, 2 * n), f32)
        for j in range(PANEL):
            inverse = 1.0 / columns[0][j][j : j + 1]
            scales = jnp.where(tall == j, inverse, scales)
            entries = [columns[0][i][j : j + 1] for i in range(PANEL)]
            pivot_row = panels[k][j : j + 1]
            for t in range(k, len(panels)):
                multiplier = columns[t - k][j] * inverse
                if t == k:
                    if j == PANEL - 1:
                        continue
                    multiplier = jnp.where(tall > j, multiplier, 0.0)
                for i in range(j + 1, PANEL):
                    columns[t - k][i] = columns[t - k][i] - multiplier * entries[i]
                panels[t] = panels[t] - multiplier * pivot_row
        panels[k] = panels[k] * jnp.sqrt(scales)
    work = jnp.concatenate(panels, axis=0)
    upper = jnp.where(col >= row, work[:, :n], 0.0)
    return upper, work[:, n:]


def weights_of(x):
    high, middle, low = (piece.astype(f32) for piece in pieces(x))
    lane = lax.broadcasted_iota(jnp.int32, x.shape, 1)
    return jnp.concatenate([jnp.where(lane < RANK, high, middle), low], axis=1).astype(bf16)


def weighted(x, weights):
    terms = dot(x, weights, NN)
    first, last = terms[:, :LANES], terms[:, LANES:]
    return first + pltpu.roll(first, RANK, 1) + last


def folded(x):
    rows = x.shape[0] // 2
    lane = lax.broadcasted_iota(jnp.int32, (rows, LANES), 1)
    return jnp.where(lane < RANK, x[:rows], x[rows:])


def unfolded(x):
    lane = lax.broadcasted_iota(jnp.int32, x.shape, 1)
    turned = pltpu.roll(x, RANK, 1)
    return jnp.concatenate([jnp.where(lane < RANK, x, turned), jnp.where(lane < RANK, turned, x)], axis=0)


def first_probes_kernel(mixing_hbm, probes_ref, out_ref, rest_ref, weights_ref, mixing_ref, tiles_ref, sems):
    part = out_ref.shape[0]
    first = pltpu.make_async_copy(mixing_hbm, mixing_ref, sems.at[2 * part])
    copies = [pltpu.make_async_copy(probes_ref.at[i], tiles_ref.at[i], sems.at[i]) for i in range(part)]
    later = [
        pltpu.make_async_copy(probes_ref.at[part + i], rest_ref.at[i], sems.at[part + i])
        for i in range(rest_ref.shape[0])
    ]
    for copy in [first] + copies + later:
        copy.start()
    first.wait()
    mixing = mixing_ref[...]
    weights = weights_of(jnp.concatenate([mixing, mixing], axis=0).T)
    weights_ref[...] = weights
    for i, copy in enumerate(copies):
        copy.wait()
        out_ref[i] = folded(weighted(tiles_ref[i], weights))
    for copy in later:
        copy.wait()


def rest_probes_kernel(rest_ref, weights_ref, out_ref):
    for i in range(out_ref.shape[0]):
        out_ref[i] = folded(weighted(rest_ref[i], weights_ref[...]))


def mixed_probes(mixing, probes):
    count, rows, width = probes.shape
    part = count // 2
    half = pltpu.VMEM((part, rows // 2, LANES), f32)
    cost = pl.CostEstimate(
        flops=2 * part * rows * width * 3 * RANK,
        bytes_accessed=part * rows * (2 * width + 4 * RANK),
        transcendentals=0,
    )
    first, rest, weights = pl.pallas_call(
        first_probes_kernel,
        out_shape=(
            half,
            pltpu.VMEM((count - part, rows, width), bf16),
            pltpu.VMEM((width, 2 * LANES), bf16),
        ),
        in_specs=[HBM, HBM],
        out_specs=(VMEM, VMEM, VMEM),
        scratch_shapes=[
            pltpu.VMEM(mixing.shape, f32),
            pltpu.VMEM((part, rows, width), bf16),
            pltpu.SemaphoreType.DMA((2 * part + 1,)),
        ],
        cost_estimate=cost,
        compiler_params=LIMIT,
        name="first_probes",
    )(mixing, probes)
    second = pl.pallas_call(
        rest_probes_kernel,
        out_shape=half,
        in_specs=[VMEM, VMEM],
        out_specs=VMEM,
        cost_estimate=cost,
        compiler_params=LIMIT,
        name="rest_probes",
    )(in_vmem(rest), in_vmem(weights))
    return [first, second]


def load_kernel(*refs):
    count = len(refs) // 2
    sems = refs[-1]
    copies = [
        pltpu.make_async_copy(refs[k], refs[count + k], sems.at[k]) for k in range(count)
    ]
    for copy in copies:
        copy.start()
    for copy in copies:
        copy.wait()


def load(meta, after, *arrays):
    def kernel(meta_ref, after_ref, *refs):
        load_kernel(*refs)

    arrays = [pltpu.with_memory_space_constraint(x, pltpu.HBM) for x in arrays]
    return pl.pallas_call(
        kernel,
        out_shape=tuple(pltpu.VMEM(x.shape, x.dtype) for x in arrays),
        in_specs=[SMEM, VMEM] + [HBM] * len(arrays),
        out_specs=(VMEM,) * len(arrays),
        scratch_shapes=[pltpu.SemaphoreType.DMA((len(arrays),))],
        cost_estimate=pl.CostEstimate(
            flops=0, bytes_accessed=2 * sum(x.size * x.dtype.itemsize for x in arrays), transcendentals=0
        ),
        compiler_params=LIMIT,
        name="load",
    )(meta, in_vmem(after), *arrays)


def sketch_kernel(
    meta_ref, own_a, own_b, moved_a, moved_b, other_a, other_b, near_ref, keep_ref, send_ref, pick_ref
):
    count = near_ref.shape[0]
    part = own_a.shape[0]
    core = meta_ref[2 * count]
    sources = (
        (own_a, 2), (own_b, 3), (moved_a, 4 * core), (moved_b, 4 * core + 1),
        (other_a, 4 - 4 * core), (other_b, 5 - 4 * core),
    )

    def pick(i):
        column = jnp.clip(meta_ref[i], 0, 6 * part - 1)
        for source, group in sources:

            @pl.when(column // part == group)
            def _():
                pick_ref[i] = source[column % part]

    for i in range(count):
        pick(i)
    for i in range(count):
        mixed = folded(weighted(near_ref[i, 0], weights_of(unfolded(pick_ref[i]))))
        mixed = jnp.where(meta_ref[count + i] > 0, mixed, 0.0)
        rows = mixed.shape[0] // 2
        keep_ref[i] = jnp.where(core == 0, mixed[:rows], mixed[rows:])
        send_ref[i] = jnp.where(core == 0, mixed[rows:], mixed[:rows])


def compress(meta, parts, near_tiles):
    count, _, rows, width = near_tiles.shape
    shape = pltpu.VMEM((count, rows // 4, LANES), f32)
    return pl.pallas_call(
        sketch_kernel,
        out_shape=(shape, shape),
        in_specs=[SMEM] + [VMEM] * 7,
        out_specs=(VMEM, VMEM),
        scratch_shapes=[pltpu.VMEM((count, rows // 2, LANES), f32)],
        cost_estimate=pl.CostEstimate(
            flops=2 * count * rows * width * 3 * RANK,
            bytes_accessed=count * rows * (2 * width + 16 * RANK),
            transcendentals=0,
        ),
        compiler_params=LIMIT,
        name="compress",
    )(meta, *[in_vmem(part) for part in parts], in_vmem(near_tiles))


def gram_kernel(terms_ref, mixed_ref, gram_ref):
    total = terms_ref[0]
    for k in range(1, terms_ref.shape[0]):
        total = total + terms_ref[k]
    mixed = total.T
    mixed_ref[...] = mixed
    first, second = mixed[:RANK], mixed[RANK:]
    gram_ref[...] = dot(first, first, NT, highest) + dot(second, second, NT, highest)


def gram_of(terms):
    return pl.pallas_call(
        gram_kernel,
        out_shape=(
            pltpu.VMEM((terms.shape[2], terms.shape[1]), f32),
            pltpu.VMEM((RANK, RANK), f32),
        ),
        in_specs=[VMEM],
        out_specs=(VMEM, VMEM),
        compiler_params=LIMIT,
        name="gram",
    )(in_vmem(terms))


def basis_kernel(core_ref, mixed_ref, gram_ref, other_ref, out_ref):
    upper, inverse = factor(gram_ref[...] + other_ref[...])
    basis = [dot(inverse, mixed_ref[k : k + RANK], NN, highest) for k in (0, RANK)]
    half = RANK // 2
    rows = jnp.where(core_ref[0] == 0, upper[:half], upper[half:])
    high, middle, low = (piece.astype(f32) for piece in pieces(rows))
    left = jnp.concatenate([high, middle], axis=0)
    right = jnp.concatenate([low, jnp.zeros_like(low)], axis=0)
    block = jnp.concatenate(basis + [left, right], axis=1).astype(bf16)
    for k in range(out_ref.shape[0]):
        out_ref[k] = block


def basis_of(core, mixed, gram, other, copies):
    return pl.pallas_call(
        basis_kernel,
        out_shape=pltpu.VMEM((copies, RANK, 2 * mixed.shape[1] + LANES), bf16),
        in_specs=[SMEM, VMEM, VMEM, VMEM],
        out_specs=VMEM,
        compiler_params=LIMIT,
        name="basis",
    )(core, in_vmem(mixed), in_vmem(gram), in_vmem(other))


def upper_half(block, width):
    half = RANK // 2
    left = block[:, width : width + RANK]
    return left[:half] + left[half:] + block[:half, width + RANK :]


def spread_kernel(far_ref, own_ref, out_ref, work_ref):
    count = own_ref.shape[0]
    groups = out_ref.shape[0] // count
    blocks = RANK // groups
    width = own_ref.shape[2] - LANES
    wide = width // LANES
    tiles = work_ref.shape[0]
    total = jnp.zeros((RANK, RANK), f32)
    for r in range(count):
        block = own_ref[r].astype(f32)
        for q in range(blocks):
            for t in range(wide):
                work_ref[q * wide + t, pl.ds(r, groups, stride=count), :] = block[
                    q * groups : (q + 1) * groups, t * LANES : (t + 1) * LANES
                ]
        upper = upper_half(block, width)
        total = total + dot(upper, upper, TN, highest)
        work_ref[tiles - 2, pl.ds(r, groups, stride=count), :] = jnp.full(
            (groups, LANES), far_ref[r].astype(f32), f32
        )
    work_ref[tiles - 1] = jnp.zeros((groups * count, LANES), f32)
    for p in range(2):
        low_row = 2 * p * groups
        packed = jnp.concatenate(
            [total[low_row : low_row + groups], total[low_row + groups : low_row + 2 * groups]], axis=1
        )
        for k, piece in enumerate(pieces(packed)):
            work_ref[tiles - 1, pl.ds(2 * k + p, groups, stride=count), :] = piece.astype(f32)
    for t in range(tiles):
        out_ref[:, t * LANES : (t + 1) * LANES] = work_ref[t].astype(bf16)


def spread(far, own, groups):
    count, _, width = own.shape
    total = RANK // groups * (width - LANES) + 2 * LANES
    return pl.pallas_call(
        spread_kernel,
        out_shape=pltpu.VMEM((groups * count, total), bf16),
        in_specs=[SMEM, VMEM],
        out_specs=VMEM,
        scratch_shapes=[pltpu.VMEM((total // LANES, groups * count, LANES), f32)],
        compiler_params=LIMIT,
        name="spread",
    )(far, in_vmem(own))


def choose_kernel(count, core_ref, own_ref, other_ref, out_ref):
    clusters, total = own_ref.shape
    body = total - 2 * LANES
    first = core_ref[0] == 0
    wanted = own_ref[:, body : body + LANES].astype(f32)
    column = lax.broadcasted_iota(jnp.int32, (clusters, clusters), 1).astype(f32)
    select = (wanted == column).astype(bf16)
    own = dot(select, own_ref[:, :body], NN)
    other = dot(select, other_ref[:, :body], NN)
    for t in range(body // LANES):
        mine, others = own[:, t * LANES : (t + 1) * LANES], other[:, t * LANES : (t + 1) * LANES]
        out_ref[:, 2 * t * LANES : (2 * t + 1) * LANES] = jnp.where(first, mine, others).astype(bf16)
        out_ref[:, (2 * t + 1) * LANES : (2 * t + 2) * LANES] = jnp.where(first, others, mine).astype(bf16)
    row = lax.broadcasted_iota(jnp.int32, (count, clusters), 0)
    column = lax.broadcasted_iota(jnp.int32, (count, clusters), 1) % count
    gather = (((column == row) | (column == row + 2) | (column == row + 4)) & (row < 2)).astype(bf16)
    sums = (dot(gather, own_ref[:, body + LANES :], NN) + dot(gather, other_ref[:, body + LANES :], NN))[:2]
    block = jnp.concatenate([piece.astype(f32) for piece in pieces(sums)] + [jnp.zeros((count - 6, LANES), f32)], axis=0)
    out_ref[:, 2 * body :] = jnp.concatenate([block] * (clusters // count), axis=0).astype(bf16)


def choose(core, own, other, count):
    rows, total = own.shape
    return pl.pallas_call(
        functools.partial(choose_kernel, count),
        out_shape=pltpu.VMEM((rows, 2 * (total - 2 * LANES) + LANES), bf16),
        in_specs=[SMEM, VMEM, VMEM],
        out_specs=VMEM,
        compiler_params=LIMIT,
        name="choose",
    )(core, in_vmem(own), in_vmem(other))


def project_kernel(core_ref, own_ref, other_ref, far_ref, out_ref, upper_ref):
    count = own_ref.shape[0]
    first = core_ref[0] == 0
    half = own_ref.shape[2] - LANES
    for i in range(count):
        mine, others = own_ref[i].astype(f32), other_ref[i].astype(f32)
        sides = (jnp.where(first, mine, others), jnp.where(first, others, mine))
        basis = [side[:, t : t + LANES] for t in range(0, half, LANES) for side in sides]
        image = dot(jnp.concatenate(basis, axis=1).astype(bf16), far_ref[i, 0], NN)
        out_ref[i] = jnp.concatenate(pieces(image), axis=0)
        upper_ref[i] = jnp.concatenate([upper_half(side, half) for side in sides], axis=0)


def project(core, own, other, far_tiles):
    count, _, rows, width = far_tiles.shape
    return pl.pallas_call(
        project_kernel,
        out_shape=(
            pltpu.VMEM((count, 3 * RANK, width), bf16),
            pltpu.VMEM((count, RANK, RANK), f32),
        ),
        in_specs=[SMEM] + [VMEM] * 3,
        out_specs=(VMEM, VMEM),
        cost_estimate=pl.CostEstimate(
            flops=2 * count * rows * width * RANK,
            bytes_accessed=count * rows * width * 4,
            transcendentals=0,
        ),
        compiler_params=LIMIT,
        name="project",
    )(core, *[in_vmem(x) for x in (own, other, far_tiles)])


def couple_kernel(scale, image_ref, upper_ref, received_ref, coupling_ref, root_ref, work_ref):
    count = image_ref.shape[0]
    rows, total = received_ref.shape
    groups = rows // count
    blocks = RANK // groups
    wide = (total - LANES) // blocks // LANES
    tiles = work_ref.shape[0]
    for t in range(tiles):
        work_ref[t] = received_ref[:, t * LANES : (t + 1) * LANES].astype(f32)
    parts = []
    for p in range(2):
        packed = sum(work_ref[tiles - 1, pl.ds(2 * k + p, groups, stride=count), :] for k in range(3))
        parts += [packed[:, :RANK], packed[:, RANK:]]
    _, inverse = factor(jnp.concatenate(parts, axis=0))
    for i in range(count):
        far = [
            jnp.concatenate(
                [work_ref[q * wide + t, pl.ds(i, groups, stride=count), :] for t in range(wide)], axis=1
            )
            for q in range(blocks)
        ]
        terms = dot(image_ref[i], jnp.concatenate(far, axis=0).astype(bf16), NT)
        coupling_ref[i, 0] = terms[:RANK] + terms[RANK : 2 * RANK] + terms[2 * RANK :]
    roots = dot(jnp.concatenate([upper_ref[i] for i in range(count)], axis=0), inverse, NT, highest) * scale
    for i in range(count):
        root_ref[i] = roots[i * RANK : (i + 1) * RANK]


def couple(image, upper, received, scale):
    count = image.shape[0]
    return pl.pallas_call(
        functools.partial(couple_kernel, scale),
        out_shape=(
            jax.ShapeDtypeStruct((count, 1, RANK, RANK), f32),
            jax.ShapeDtypeStruct((count, RANK, RANK), f32),
        ),
        in_specs=[VMEM] * 3,
        out_specs=(VMEM, VMEM),
        scratch_shapes=[pltpu.VMEM((received.shape[1] // LANES, received.shape[0], LANES), f32)],
        compiler_params=LIMIT,
        name="couple",
    )(*[in_vmem(x) for x in (image, upper, received)])


def shards(near_tiles, near_cols, near_count, probes, mixing, far_tiles, far_cols):
    count = probes.shape[0]
    subtrees = lax.axis_size("leaf")
    members = lax.axis_size("blk")
    leaf_pos = lax.axis_index("leaf")
    blk_pos = lax.axis_index("blk")
    core = blk_pos % 2
    pair = [(i, i ^ 1) for i in range(members)]
    lanes = [list(range(c, members, 2)) for c in range(2)]
    shift = [
        (g * members + b, (g + step) * members + b)
        for g in range(subtrees)
        for b in range(members)
        for step in [1 - 2 * (b % 2)]
        if 0 <= g + step < subtrees
    ]

    core = core.reshape(1).astype(jnp.int32)
    live = (blk_pos < near_count).astype(jnp.int32)
    near_meta = jnp.concatenate([near_cols[:, 0] - (leaf_pos * count - REACH), live, core])

    mixing, probes = (pltpu.with_memory_space_constraint(x, pltpu.HBM) for x in (mixing.T, probes))
    own = mixed_probes(mixing, probes)
    moved = [lax.ppermute(x, ("leaf", "blk"), shift) for x in own]
    (near_tiles,) = load(near_meta, own[1], near_tiles)
    other = lax.ppermute(moved[0], "blk", pair)
    moved[1], near_tiles, other = lax.optimization_barrier((moved[1], near_tiles, other))
    other = [other, lax.ppermute(moved[1], "blk", pair)]
    keep, send = compress(near_meta, own + moved + other, near_tiles)
    halves = keep + lax.ppermute(send, "blk", pair)
    terms = lax.all_to_all(halves, "blk", 0, 0, tiled=True, axis_index_groups=lanes)
    mixed, gram = gram_of(terms)
    own = basis_of(core, mixed, gram, lax.ppermute(gram, "blk", pair), count)
    own = lax.all_to_all(own, "blk", 0, 0, tiled=True, axis_index_groups=lanes)
    other = lax.ppermute(own, "blk", pair)
    payload = spread(far_cols[:, 0], own, subtrees)
    slices = lax.all_to_all(payload.reshape(subtrees, count, -1), "leaf", 0, 0, tiled=True)
    slices = slices.reshape(payload.shape)
    image, upper = project(core, own, other, far_tiles)
    chosen = choose(core, slices, lax.ppermute(slices, "blk", pair), count)
    received = lax.all_to_all(chosen.reshape(subtrees, count, -1), "leaf", 0, 0, tiled=True)
    scale = math.sqrt(subtrees * count * RANK)
    return couple(image, upper, received.reshape(chosen.shape), scale)


def solution(mesh):
    in_specs = (
        P("leaf", "blk", None, None),
        P("leaf", "blk"),
        P("leaf"),
        P("leaf", None, None),
        P(),
        P("leaf", "blk", None, None),
        P("leaf", "blk"),
    )
    out_specs = (P("leaf", "blk", None, None), P("leaf", None, None))
    return jax.shard_map(shards, mesh=mesh, in_specs=in_specs, out_specs=out_specs, check_vma=False)
```

```python
import functools
import math

import jax
import jax.numpy as jnp
from jax import lax
from jax.experimental import pallas as pl
from jax.experimental.pallas import tpu as pltpu
from jax.sharding import PartitionSpec as P

RANK = 64
REACH = 8
LANES = 128
PANEL = 8

f32 = jnp.float32
bf16 = jnp.bfloat16
highest = lax.Precision.HIGHEST

HBM = pl.BlockSpec(memory_space=pltpu.HBM)
SMEM = pl.BlockSpec(memory_space=pltpu.SMEM)
VMEM = pl.BlockSpec(memory_space=pltpu.VMEM)

LIMIT = pltpu.CompilerParams(vmem_limit_bytes=24 << 20)

NN = (((1,), (0,)), ((), ()))
NT = (((1,), (1,)), ((), ()))
TN = (((0,), (0,)), ((), ()))


def dot(a, b, dims, precision=None):
    return lax.dot_general(a, b, dims, precision=precision, preferred_element_type=f32)


def pieces(x):
    high = x.astype(bf16)
    rest = x - high.astype(f32)
    middle = rest.astype(bf16)
    low = (rest - middle.astype(f32)).astype(bf16)
    return high, middle, low


def in_vmem(x):
    return pltpu.with_memory_space_constraint(x, pltpu.VMEM)


def factor(gram):
    n = gram.shape[0]
    row = lax.broadcasted_iota(jnp.int32, (n, n), 0)
    col = lax.broadcasted_iota(jnp.int32, (n, n), 1)
    tall = lax.broadcasted_iota(jnp.int32, (PANEL, 2 * n), 0)
    work = jnp.concatenate([gram, (row == col).astype(f32)], axis=1)
    panels = [work[k : k + PANEL] for k in range(0, n, PANEL)]
    for k in range(len(panels)):
        columns = [
            [
                jnp.broadcast_to(panels[t][:, k * PANEL + j : k * PANEL + j + 1], (PANEL, 2 * n))
                for j in range(PANEL)
            ]
            for t in range(k, len(panels))
        ]
        scales = jnp.zeros((PANEL, 2 * n), f32)
        for j in range(PANEL):
            inverse = 1.0 / columns[0][j][j : j + 1]
            scales = jnp.where(tall == j, inverse, scales)
            entries = [columns[0][i][j : j + 1] for i in range(PANEL)]
            pivot_row = panels[k][j : j + 1]
            for t in range(k, len(panels)):
                multiplier = columns[t - k][j] * inverse
                if t == k:
                    if j == PANEL - 1:
                        continue
                    multiplier = jnp.where(tall > j, multiplier, 0.0)
                for i in range(j + 1, PANEL):
                    columns[t - k][i] = columns[t - k][i] - multiplier * entries[i]
                panels[t] = panels[t] - multiplier * pivot_row
        panels[k] = panels[k] * jnp.sqrt(scales)
    work = jnp.concatenate(panels, axis=0)
    upper = jnp.where(col >= row, work[:, :n], 0.0)
    return upper, work[:, n:]


def weights_of(x):
    high, middle, low = (piece.astype(f32) for piece in pieces(x))
    lane = lax.broadcasted_iota(jnp.int32, x.shape, 1)
    return jnp.concatenate([jnp.where(lane < RANK, high, middle), low], axis=1).astype(bf16)


def weighted(x, weights):
    terms = dot(x, weights, NN)
    first, last = terms[:, :LANES], terms[:, LANES:]
    return first + pltpu.roll(first, RANK, 1) + last


def folded(x):
    rows = x.shape[0] // 2
    lane = lax.broadcasted_iota(jnp.int32, (rows, LANES), 1)
    return jnp.where(lane < RANK, x[:rows], x[rows:])


def unfolded(x):
    lane = lax.broadcasted_iota(jnp.int32, x.shape, 1)
    turned = pltpu.roll(x, RANK, 1)
    return jnp.concatenate([jnp.where(lane < RANK, x, turned), jnp.where(lane < RANK, turned, x)], axis=0)


def first_probes_kernel(mixing_hbm, probes_ref, out_ref, rest_ref, weights_ref, mixing_ref, tiles_ref, sems):
    part = out_ref.shape[0]
    first = pltpu.make_async_copy(mixing_hbm, mixing_ref, sems.at[2 * part])
    copies = [pltpu.make_async_copy(probes_ref.at[i], tiles_ref.at[i], sems.at[i]) for i in range(part)]
    later = [
        pltpu.make_async_copy(probes_ref.at[part + i], rest_ref.at[i], sems.at[part + i])
        for i in range(rest_ref.shape[0])
    ]
    for copy in [first] + copies + later:
        copy.start()
    first.wait()
    mixing = mixing_ref[...]
    weights = weights_of(jnp.concatenate([mixing, mixing], axis=0).T)
    weights_ref[...] = weights
    for i, copy in enumerate(copies):
        copy.wait()
        out_ref[i] = folded(weighted(tiles_ref[i], weights))
    for copy in later:
        copy.wait()


def rest_probes_kernel(rest_ref, weights_ref, out_ref):
    for i in range(out_ref.shape[0]):
        out_ref[i] = folded(weighted(rest_ref[i], weights_ref[...]))


def mixed_probes(mixing, probes):
    count, rows, width = probes.shape
    part = count // 2
    half = pltpu.VMEM((part, rows // 2, LANES), f32)
    cost = pl.CostEstimate(
        flops=2 * part * rows * width * 3 * RANK,
        bytes_accessed=part * rows * (2 * width + 4 * RANK),
        transcendentals=0,
    )
    first, rest, weights = pl.pallas_call(
        first_probes_kernel,
        out_shape=(
            half,
            pltpu.VMEM((count - part, rows, width), bf16),
            pltpu.VMEM((width, 2 * LANES), bf16),
        ),
        in_specs=[HBM, HBM],
        out_specs=(VMEM, VMEM, VMEM),
        scratch_shapes=[
            pltpu.VMEM(mixing.shape, f32),
            pltpu.VMEM((part, rows, width), bf16),
            pltpu.SemaphoreType.DMA((2 * part + 1,)),
        ],
        cost_estimate=cost,
        compiler_params=LIMIT,
        name="first_probes",
    )(mixing, probes)
    second = pl.pallas_call(
        rest_probes_kernel,
        out_shape=half,
        in_specs=[VMEM, VMEM],
        out_specs=VMEM,
        cost_estimate=cost,
        compiler_params=LIMIT,
        name="rest_probes",
    )(in_vmem(rest), in_vmem(weights))
    return [first, second]


def load_kernel(*refs):
    count = len(refs) // 2
    sems = refs[-1]
    copies = [
        pltpu.make_async_copy(refs[k], refs[count + k], sems.at[k]) for k in range(count)
    ]
    for copy in copies:
        copy.start()
    for copy in copies:
        copy.wait()


def load(meta, after, *arrays):
    def kernel(meta_ref, after_ref, *refs):
        load_kernel(*refs)

    arrays = [pltpu.with_memory_space_constraint(x, pltpu.HBM) for x in arrays]
    return pl.pallas_call(
        kernel,
        out_shape=tuple(pltpu.VMEM(x.shape, x.dtype) for x in arrays),
        in_specs=[SMEM, VMEM] + [HBM] * len(arrays),
        out_specs=(VMEM,) * len(arrays),
        scratch_shapes=[pltpu.SemaphoreType.DMA((len(arrays),))],
        cost_estimate=pl.CostEstimate(
            flops=0, bytes_accessed=2 * sum(x.size * x.dtype.itemsize for x in arrays), transcendentals=0
        ),
        compiler_params=LIMIT,
        name="load",
    )(meta, in_vmem(after), *arrays)


def sketch_kernel(
    meta_ref, own_a, own_b, moved_a, moved_b, other_a, other_b, near_ref, keep_ref, send_ref, pick_ref
):
    count = near_ref.shape[0]
    part = own_a.shape[0]
    core = meta_ref[2 * count]
    sources = (
        (own_a, 2), (own_b, 3), (moved_a, 4 * core), (moved_b, 4 * core + 1),
        (other_a, 4 - 4 * core), (other_b, 5 - 4 * core),
    )

    def pick(i):
        column = jnp.clip(meta_ref[i], 0, 6 * part - 1)
        for source, group in sources:

            @pl.when(column // part == group)
            def _():
                pick_ref[i] = source[column % part]

    for i in range(count):
        pick(i)
    for i in range(count):
        mixed = folded(weighted(near_ref[i, 0], weights_of(unfolded(pick_ref[i]))))
        mixed = jnp.where(meta_ref[count + i] > 0, mixed, 0.0)
        rows = mixed.shape[0] // 2
        keep_ref[i] = jnp.where(core == 0, mixed[:rows], mixed[rows:])
        send_ref[i] = jnp.where(core == 0, mixed[rows:], mixed[:rows])


def compress(meta, parts, near_tiles):
    count, _, rows, width = near_tiles.shape
    shape = pltpu.VMEM((count, rows // 4, LANES), f32)
    return pl.pallas_call(
        sketch_kernel,
        out_shape=(shape, shape),
        in_specs=[SMEM] + [VMEM] * 7,
        out_specs=(VMEM, VMEM),
        scratch_shapes=[pltpu.VMEM((count, rows // 2, LANES), f32)],
        cost_estimate=pl.CostEstimate(
            flops=2 * count * rows * width * 3 * RANK,
            bytes_accessed=count * rows * (2 * width + 16 * RANK),
            transcendentals=0,
        ),
        compiler_params=LIMIT,
        name="compress",
    )(meta, *[in_vmem(part) for part in parts], in_vmem(near_tiles))


def gram_kernel(terms_ref, mixed_ref, gram_ref):
    total = terms_ref[0]
    for k in range(1, terms_ref.shape[0]):
        total = total + terms_ref[k]
    mixed = total.T
    mixed_ref[...] = mixed
    first, second = mixed[:RANK], mixed[RANK:]
    gram_ref[...] = dot(first, first, NT, highest) + dot(second, second, NT, highest)


def gram_of(terms):
    return pl.pallas_call(
        gram_kernel,
        out_shape=(
            pltpu.VMEM((terms.shape[2], terms.shape[1]), f32),
            pltpu.VMEM((RANK, RANK), f32),
        ),
        in_specs=[VMEM],
        out_specs=(VMEM, VMEM),
        compiler_params=LIMIT,
        name="gram",
    )(in_vmem(terms))


def basis_kernel(core_ref, mixed_ref, gram_ref, other_ref, out_ref):
    upper, inverse = factor(gram_ref[...] + other_ref[...])
    basis = [dot(inverse, mixed_ref[k : k + RANK], NN, highest) for k in (0, RANK)]
    half = RANK // 2
    rows = jnp.where(core_ref[0] == 0, upper[:half], upper[half:])
    high, middle, low = (piece.astype(f32) for piece in pieces(rows))
    left = jnp.concatenate([high, middle], axis=0)
    right = jnp.concatenate([low, jnp.zeros_like(low)], axis=0)
    block = jnp.concatenate(basis + [left, right], axis=1).astype(bf16)
    for k in range(out_ref.shape[0]):
        out_ref[k] = block


def basis_of(core, mixed, gram, other, copies):
    return pl.pallas_call(
        basis_kernel,
        out_shape=pltpu.VMEM((copies, RANK, 2 * mixed.shape[1] + LANES), bf16),
        in_specs=[SMEM, VMEM, VMEM, VMEM],
        out_specs=VMEM,
        compiler_params=LIMIT,
        name="basis",
    )(core, in_vmem(mixed), in_vmem(gram), in_vmem(other))


def upper_half(block, width):
    half = RANK // 2
    left = block[:, width : width + RANK]
    return left[:half] + left[half:] + block[:half, width + RANK :]


def spread_kernel(far_ref, own_ref, out_ref, work_ref):
    count = own_ref.shape[0]
    groups = out_ref.shape[0] // count
    blocks = RANK // groups
    width = own_ref.shape[2] - LANES
    wide = width // LANES
    tiles = work_ref.shape[0]
    uppers = []
    for r in range(count):
        block = own_ref[r].astype(f32)
        for q in range(blocks):
            for t in range(wide):
                work_ref[q * wide + t, pl.ds(r, groups, stride=count), :] = block[
                    q * groups : (q + 1) * groups, t * LANES : (t + 1) * LANES
                ]
        uppers.append(upper_half(block, width))
        work_ref[tiles - 2, pl.ds(r, groups, stride=count), :] = jnp.full(
            (groups, LANES), far_ref[r].astype(f32), f32
        )
    uppers = jnp.concatenate(uppers, axis=0)
    total = dot(uppers, uppers, TN, highest)
    work_ref[tiles - 1] = jnp.zeros((groups * count, LANES), f32)
    for p in range(2):
        low_row = 2 * p * groups
        packed = jnp.concatenate(
            [total[low_row : low_row + groups], total[low_row + groups : low_row + 2 * groups]], axis=1
        )
        for k, piece in enumerate(pieces(packed)):
            work_ref[tiles - 1, pl.ds(2 * k + p, groups, stride=count), :] = piece.astype(f32)
    for t in range(tiles):
        out_ref[:, t * LANES : (t + 1) * LANES] = work_ref[t].astype(bf16)


def spread(far, own, groups):
    count, _, width = own.shape
    total = RANK // groups * (width - LANES) + 2 * LANES
    return pl.pallas_call(
        spread_kernel,
        out_shape=pltpu.VMEM((groups * count, total), bf16),
        in_specs=[SMEM, VMEM],
        out_specs=VMEM,
        scratch_shapes=[pltpu.VMEM((total // LANES, groups * count, LANES), f32)],
        compiler_params=LIMIT,
        name="spread",
    )(far, in_vmem(own))


def choose_kernel(count, core_ref, own_ref, other_ref, out_ref):
    clusters, total = own_ref.shape
    body = total - 2 * LANES
    first = core_ref[0] == 0
    wanted = own_ref[:, body : body + LANES].astype(f32)
    column = lax.broadcasted_iota(jnp.int32, (clusters, clusters), 1).astype(f32)
    select = (wanted == column).astype(bf16)
    own = dot(select, own_ref[:, :body], NN)
    other = dot(select, other_ref[:, :body], NN)
    for t in range(body // LANES):
        mine, others = own[:, t * LANES : (t + 1) * LANES], other[:, t * LANES : (t + 1) * LANES]
        out_ref[:, 2 * t * LANES : (2 * t + 1) * LANES] = jnp.where(first, mine, others).astype(bf16)
        out_ref[:, (2 * t + 1) * LANES : (2 * t + 2) * LANES] = jnp.where(first, others, mine).astype(bf16)
    row = lax.broadcasted_iota(jnp.int32, (count, clusters), 0)
    column = lax.broadcasted_iota(jnp.int32, (count, clusters), 1) % count
    gather = (((column == row) | (column == row + 2) | (column == row + 4)) & (row < 2)).astype(bf16)
    sums = (dot(gather, own_ref[:, body + LANES :], NN) + dot(gather, other_ref[:, body + LANES :], NN))[:2]
    block = jnp.concatenate([piece.astype(f32) for piece in pieces(sums)] + [jnp.zeros((count - 6, LANES), f32)], axis=0)
    out_ref[:, 2 * body :] = jnp.concatenate([block] * (clusters // count), axis=0).astype(bf16)


def choose(core, own, other, count):
    rows, total = own.shape
    return pl.pallas_call(
        functools.partial(choose_kernel, count),
        out_shape=pltpu.VMEM((rows, 2 * (total - 2 * LANES) + LANES), bf16),
        in_specs=[SMEM, VMEM, VMEM],
        out_specs=VMEM,
        compiler_params=LIMIT,
        name="choose",
    )(core, in_vmem(own), in_vmem(other))


def project_kernel(core_ref, own_ref, other_ref, far_ref, out_ref, upper_ref):
    count = own_ref.shape[0]
    first = core_ref[0] == 0
    half = own_ref.shape[2] - LANES
    for i in range(count):
        mine, others = own_ref[i].astype(f32), other_ref[i].astype(f32)
        sides = (jnp.where(first, mine, others), jnp.where(first, others, mine))
        basis = [side[:, t : t + LANES] for t in range(0, half, LANES) for side in sides]
        image = dot(jnp.concatenate(basis, axis=1).astype(bf16), far_ref[i, 0], NN)
        out_ref[i] = jnp.concatenate(pieces(image), axis=0)
        upper_ref[i] = jnp.concatenate([upper_half(side, half) for side in sides], axis=0)


def project(core, own, other, far_tiles):
    count, _, rows, width = far_tiles.shape
    return pl.pallas_call(
        project_kernel,
        out_shape=(
            pltpu.VMEM((count, 3 * RANK, width), bf16),
            pltpu.VMEM((count, RANK, RANK), f32),
        ),
        in_specs=[SMEM] + [VMEM] * 3,
        out_specs=(VMEM, VMEM),
        cost_estimate=pl.CostEstimate(
            flops=2 * count * rows * width * RANK,
            bytes_accessed=count * rows * width * 4,
            transcendentals=0,
        ),
        compiler_params=LIMIT,
        name="project",
    )(core, *[in_vmem(x) for x in (own, other, far_tiles)])


def couple_kernel(scale, image_ref, upper_ref, received_ref, coupling_ref, root_ref, work_ref):
    count = image_ref.shape[0]
    rows, total = received_ref.shape
    groups = rows // count
    blocks = RANK // groups
    wide = (total - LANES) // blocks // LANES
    tiles = work_ref.shape[0]
    for t in range(tiles):
        work_ref[t] = received_ref[:, t * LANES : (t + 1) * LANES].astype(f32)
    parts = []
    for p in range(2):
        packed = sum(work_ref[tiles - 1, pl.ds(2 * k + p, groups, stride=count), :] for k in range(3))
        parts += [packed[:, :RANK], packed[:, RANK:]]
    _, inverse = factor(jnp.concatenate(parts, axis=0))
    for i in range(count):
        far = [
            jnp.concatenate(
                [work_ref[q * wide + t, pl.ds(i, groups, stride=count), :] for t in range(wide)], axis=1
            )
            for q in range(blocks)
        ]
        terms = dot(image_ref[i], jnp.concatenate(far, axis=0).astype(bf16), NT)
        coupling_ref[i, 0] = terms[:RANK] + terms[RANK : 2 * RANK] + terms[2 * RANK :]
    roots = dot(jnp.concatenate([upper_ref[i] for i in range(count)], axis=0), inverse, NT, highest) * scale
    for i in range(count):
        root_ref[i] = roots[i * RANK : (i + 1) * RANK]


def couple(image, upper, received, scale):
    count = image.shape[0]
    return pl.pallas_call(
        functools.partial(couple_kernel, scale),
        out_shape=(
            jax.ShapeDtypeStruct((count, 1, RANK, RANK), f32),
            jax.ShapeDtypeStruct((count, RANK, RANK), f32),
        ),
        in_specs=[VMEM] * 3,
        out_specs=(VMEM, VMEM),
        scratch_shapes=[pltpu.VMEM((received.shape[1] // LANES, received.shape[0], LANES), f32)],
        compiler_params=LIMIT,
        name="couple",
    )(*[in_vmem(x) for x in (image, upper, received)])


def shards(near_tiles, near_cols, near_count, probes, mixing, far_tiles, far_cols):
    count = probes.shape[0]
    subtrees = lax.axis_size("leaf")
    members = lax.axis_size("blk")
    leaf_pos = lax.axis_index("leaf")
    blk_pos = lax.axis_index("blk")
    core = blk_pos % 2
    pair = [(i, i ^ 1) for i in range(members)]
    lanes = [list(range(c, members, 2)) for c in range(2)]
    shift = [
        (g * members + b, (g + step) * members + b)
        for g in range(subtrees)
        for b in range(members)
        for step in [1 - 2 * (b % 2)]
        if 0 <= g + step < subtrees
    ]

    core = core.reshape(1).astype(jnp.int32)
    live = (blk_pos < near_count).astype(jnp.int32)
    near_meta = jnp.concatenate([near_cols[:, 0] - (leaf_pos * count - REACH), live, core])

    mixing, probes = (pltpu.with_memory_space_constraint(x, pltpu.HBM) for x in (mixing.T, probes))
    own = mixed_probes(mixing, probes)
    moved = [lax.ppermute(x, ("leaf", "blk"), shift) for x in own]
    (near_tiles,) = load(near_meta, own[1], near_tiles)
    other = lax.ppermute(moved[0], "blk", pair)
    moved[1], near_tiles, other = lax.optimization_barrier((moved[1], near_tiles, other))
    other = [other, lax.ppermute(moved[1], "blk", pair)]
    keep, send = compress(near_meta, own + moved + other, near_tiles)
    halves = keep + lax.ppermute(send, "blk", pair)
    terms = lax.all_to_all(halves, "blk", 0, 0, tiled=True, axis_index_groups=lanes)
    mixed, gram = gram_of(terms)
    own = basis_of(core, mixed, gram, lax.ppermute(gram, "blk", pair), count)
    own = lax.all_to_all(own, "blk", 0, 0, tiled=True, axis_index_groups=lanes)
    other = lax.ppermute(own, "blk", pair)
    payload = spread(far_cols[:, 0], own, subtrees)
    slices = lax.all_to_all(payload.reshape(subtrees, count, -1), "leaf", 0, 0, tiled=True)
    slices = slices.reshape(payload.shape)
    image, upper = project(core, own, other, far_tiles)
    chosen = choose(core, slices, lax.ppermute(slices, "blk", pair), count)
    received = lax.all_to_all(chosen.reshape(subtrees, count, -1), "leaf", 0, 0, tiled=True)
    scale = math.sqrt(subtrees * count * RANK)
    return couple(image, upper, received.reshape(chosen.shape), scale)


def solution(mesh):
    in_specs = (
        P("leaf", "blk", None, None),
        P("leaf", "blk"),
        P("leaf"),
        P("leaf", None, None),
        P(),
        P("leaf", "blk", None, None),
        P("leaf", "blk"),
    )
    out_specs = (P("leaf", "blk", None, None), P("leaf", None, None))
    return jax.shard_map(shards, mesh=mesh, in_specs=in_specs, out_specs=out_specs, check_vma=False)
```
